32 devices in a mesh: ra: 4 (over x, core), rb: 8 (over z, y).
Axes of the slice: x: 2, y: 2, z: 4, core: 2. Of those that a mesh axis runs over, the one named last changes fastest.
Arguments:
- amplitude: bfloat16 [2, 512, 512, 256], P(None, 'ra', 'rb'), may hold values from -6 to 6
- coupling: bfloat16 [6, 256, 256], replicated, may hold values from -0.5 to 0.5
- pattern: int32 [6, 4, 4], replicated, may hold values 0 or 1
- radial: float32 [6, 512, 512], P(None, 'ra', 'rb'), may hold values from -2.4 to 2.4
- first_prop: bfloat16 [2, 512, 512], replicated, may hold values from -0.1875 to 0.1875
- second_prop: bfloat16 [2, 512, 512], replicated, may hold values from -0.1875 to 0.1875
Outputs:
- evolved: bfloat16 [2, 512, 512, 256], P(None, 'ra', 'rb')
The draws below stay inside these ranges and needn't reach their ends.
All inputs are finite; a program needn't handle non-finite values.
Results may differ from the reference program's by a relative error of at most 0.0095.
Values may be sent and summed in bfloat16 or wider, within the bound.
A program may use at most 128 MiB of HBM per device.

```python
import jax
import jax.numpy as jnp
from jax import lax

C = 256
BS = 64
NB = 4
KTERMS = 6
N1 = 512
N2 = 512
STEPS = 2


def place_ends(result, key, least, high):
    spot = [jax.random.randint(jax.random.fold_in(key, axis), (), 0, length) for axis, length in enumerate(result.shape)]
    main_axis = result.shape.index(max(result.shape))
    beside = spot[:main_axis] + [(spot[main_axis] + 1) % result.shape[main_axis]] + spot[main_axis + 1:]
    return result.at[tuple(spot)].set(least).at[tuple(beside)].set(high)


def levels(key, shape, cuts, low, largest):
    factor_of = 1.0
    for dim, parts in cuts:
        heights = jax.random.uniform(jax.random.fold_in(jax.random.fold_in(key, 6), dim), (parts,), jnp.float32, low / len(cuts), largest / len(cuts))
        factor_of = factor_of * jnp.repeat(jnp.exp(heights), shape[dim] // parts).reshape((-1,) + (1,) * (len(shape) - 1 - dim))
    return factor_of


def centred(own_key, shape, scale, bound, shards=(), held_as=jnp.bfloat16):
    factor_of = levels(own_key, shape, shards, -0.22, 0.18) if shards else 1.0
    result = jax.random.normal(own_key, shape, jnp.float32) * scale * factor_of
    return jnp.minimum(jnp.maximum(result, -bound), bound).astype(held_as)


def setup_inputs(seed: int = 0) -> dict:
    splits = jax.random.split(jax.random.key(seed), 7)
    amplitude = centred(splits[0], (2, N1, N2, C), 1.0, 6.0, ((1, 4), (2, 8)))
    coupling = centred(splits[1], (KTERMS, C, C), (C // 2) ** -0.5, 0.5)
    pattern = place_ends((jax.random.randint(splits[2], (KTERMS, NB, NB), 0, 2) < 1).astype(jnp.int32), jax.random.fold_in(splits[2], 1), 0, 1)
    radial = centred(splits[3], (KTERMS, N1, N2), 0.4, 2.4, ((1, 4), (2, 8)), jnp.float32)
    first_prop = centred(splits[4], (2, N1, N1), (2 * N1) ** -0.5, 0.1875)
    second_prop = centred(splits[5], (2, N2, N2), (2 * N2) ** -0.5, 0.1875)
    return dict(amplitude=amplitude, coupling=coupling, pattern=pattern, radial=radial, first_prop=first_prop, second_prop=second_prop)


def spread_mask(pattern):
    blocks = pattern.astype(jnp.float32)
    terms, count = blocks.shape[0], blocks.shape[1]
    spread = jnp.broadcast_to(blocks[:, :, None, :, None], (terms, count, BS, count, BS))
    return spread.reshape(terms, count * BS, count * BS)


def couple(amplitude, coupling, block_mask, radial):
    wide = amplitude.astype(jnp.float32)

    def add_term(multipole, summed):
        weights = coupling[multipole].astype(jnp.float32) * block_mask[multipole]
        applied = jnp.einsum("ij,xabj->xabi", weights, wide)
        return summed + applied * radial[multipole][None, :, :, None]

    coupled = lax.fori_loop(0, KTERMS, add_term, jnp.zeros(amplitude.shape, jnp.float32))
    return jnp.stack([wide[0] + coupled[1], wide[1] - coupled[0]]).astype(jnp.bfloat16)


def along_first(amplitude, propagator):
    wide = amplitude.astype(jnp.float32)
    matrix = propagator.astype(jnp.float32)
    real_part = jnp.einsum("ac,cbi->abi", matrix[0], wide[0]) - jnp.einsum("ac,cbi->abi", matrix[1], wide[1])
    imag_part = jnp.einsum("ac,cbi->abi", matrix[0], wide[1]) + jnp.einsum("ac,cbi->abi", matrix[1], wide[0])
    return jnp.stack([real_part, imag_part]).astype(jnp.bfloat16)


def along_second(amplitude, propagator):
    wide = amplitude.astype(jnp.float32)
    matrix = propagator.astype(jnp.float32)
    real_part = jnp.einsum("bc,aci->abi", matrix[0], wide[0]) - jnp.einsum("bc,aci->abi", matrix[1], wide[1])
    imag_part = jnp.einsum("bc,aci->abi", matrix[0], wide[1]) + jnp.einsum("bc,aci->abi", matrix[1], wide[0])
    return jnp.stack([real_part, imag_part]).astype(jnp.bfloat16)


def reference(amplitude, coupling, pattern, radial, first_prop, second_prop):
    block_mask = spread_mask(pattern)
    for sweep in range(STEPS):
        kicked = couple(amplitude, coupling, block_mask, radial)
        half = along_first(kicked, first_prop)
        amplitude = along_second(half, second_prop)
    return amplitude
```

```python
import functools

import jax
import jax.numpy as jnp
from jax import lax
from jax.experimental import pallas as pl
from jax.experimental.pallas import tpu as pltpu
from jax.sharding import PartitionSpec as P

KTERMS = 6
STEPS = 2
LANES = 128
TILE = 16
HALF = 8
MESH = pl.DeviceIdType.MESH


def complex_rows(matrix, piece):
    form = "ac,cqw->aqw"
    real_part = jnp.einsum(
        form, matrix[0], piece[0], preferred_element_type=jnp.float32
    ) - jnp.einsum(form, matrix[1], piece[1], preferred_element_type=jnp.float32)
    imag_part = jnp.einsum(
        form, matrix[0], piece[1], preferred_element_type=jnp.float32
    ) + jnp.einsum(form, matrix[1], piece[0], preferred_element_type=jnp.float32)
    return jnp.stack([real_part, imag_part]).astype(jnp.bfloat16)


def masked_weights(coupling, pattern):
    channels = coupling.shape[1]
    count = pattern.shape[1]
    block_size = channels // count
    spread = jnp.broadcast_to(
        pattern[:, :, None, :, None], (KTERMS, count, block_size, count, block_size)
    )
    return coupling * spread.reshape(KTERMS, channels, channels).astype(jnp.bfloat16)


def plain(amplitude, coupling, pattern, radial, first_prop, second_prop):
    first_rows, second_rows, channels = (amplitude.shape[1], amplitude.shape[2], amplitude.shape[3])
    cells = first_rows * second_rows
    groups_a = lax.axis_size("ra")
    groups_b = lax.axis_size("rb")
    width_a = channels // groups_a
    width_b = channels // groups_b
    weights = masked_weights(coupling, pattern)
    radial_cells = radial.reshape(KTERMS, cells).T
    for sweep in range(STEPS):
        flat = amplitude.reshape(2 * cells, channels)
        applied = jnp.einsum("mj,kij->mki", flat, weights, preferred_element_type=jnp.float32)
        applied = applied.reshape(2, cells, KTERMS, channels)
        coupled = jnp.sum(applied * radial_cells[None, :, :, None], axis=2)
        wide = amplitude.reshape(2, cells, channels).astype(jnp.float32)
        kicked = jnp.stack([wide[0] + coupled[1], wide[1] - coupled[0]]).astype(jnp.bfloat16)
        grouped = kicked.reshape(2, first_rows, second_rows, groups_a, width_a)
        grouped = grouped.transpose(0, 1, 3, 2, 4).reshape(
            2, first_rows, groups_a, second_rows * width_a
        )
        half = complex_rows(
            first_prop, lax.all_to_all(grouped, "ra", split_axis=2, concat_axis=1, tiled=True)
        )
        restored = lax.all_to_all(half, "ra", split_axis=1, concat_axis=2, tiled=True)
        restored = restored.reshape(2, first_rows, groups_a, second_rows, width_a)
        restored = restored.transpose(0, 1, 3, 2, 4).reshape(
            2, first_rows, second_rows, groups_b, width_b
        )
        regrouped = restored.transpose(0, 2, 3, 1, 4).reshape(
            2, second_rows, groups_b, first_rows * width_b
        )
        moved = complex_rows(
            second_prop, lax.all_to_all(regrouped, "rb", split_axis=2, concat_axis=1, tiled=True)
        )
        settled = lax.all_to_all(moved, "rb", split_axis=1, concat_axis=2, tiled=True)
        settled = settled.reshape(2, second_rows, groups_b, first_rows, width_b)
        amplitude = settled.transpose(0, 3, 1, 2, 4).reshape(2, first_rows, second_rows, channels)
    return amplitude


def flip(value, mask, bits):
    out = 0
    for n in range(bits):
        weight = 1 << n
        out = out + lax.rem(lax.div(value, weight) + lax.div(mask, weight), 2) * weight
    return out


def fused_kernel(ra, rb, amp_ref, weights_ref, radial_ref, first_ref, second_ref, out_ref,
                 lower, upper, left, right, turn, stage, first_mat, second_mat, near, far,
                 load_sem, store_sem, send_sem, recv_near, recv_far, recv_back, recv_home, rad_send, rad_recv):
    at_a, at_b = lax.axis_index("ra"), lax.axis_index("rb")
    bits_a, bits_b = ra.bit_length() - 1, rb.bit_length() - 1
    chunks = left.shape[1]
    pairs = left.shape[2]
    groups = left.shape[3]
    own = groups // (2 * ra)
    per = pairs * 2
    depth = first_ref.shape[1]
    halfway = lower.shape[1] // 2
    channels = lower.shape[4]
    a_tiles = lower.shape[2]
    devices = ra * rb
    route = [("b", n) for n in reversed(range(bits_b))]
    route = [("b", bits_b - 1), ("a", bits_a - 1)] + [("b", n) for n in range(bits_b - 1)] + [("a", n) for n in range(bits_a - 1)]

    def partner(d):
        mask_a, mask_b = 0, 0
        for n, (axis, bit) in enumerate(route):
            one = lax.rem(lax.div(d, 1 << n), 2) * (1 << bit)
            if axis == "a":
                mask_a = mask_a + one
            else:
                mask_b = mask_b + one
        return flip(at_a, mask_a, bits_a), flip(at_b, mask_b, bits_b)

    barrier = pltpu.get_barrier_semaphore()

    def greet(d, carry):
        to_a, to_b = partner(d)
        pl.semaphore_signal(barrier, inc=1, device_id=(to_a, to_b), device_id_type=MESH)
        return carry

    lax.fori_loop(1, devices, greet, 0)

    def load(q):
        slot = lax.rem(q, 2)
        return pltpu.make_async_copy(amp_ref.at[:, :, pl.ds(q * TILE, TILE)], stage.at[slot], load_sem.at[slot])

    def store(q):
        slot = lax.rem(q, 2)
        return pltpu.make_async_copy(stage.at[slot], out_ref.at[:, :, pl.ds(q * TILE, TILE)], store_sem.at[slot])

    load(jnp.int32(0)).start()
    load(jnp.int32(1)).start()

    for source, target in ((first_ref, first_mat), (second_ref, second_mat)):
        target[:depth, :depth] = source[0]
        target[depth:, depth:] = source[0]
        target[:depth, depth:] = -source[1]
        target[depth:, :depth] = source[1]

    b_rows = amp_ref.shape[2]

    def lay(g, carry):
        block = radial_ref[pl.ds(g * HALF, HALF)].reshape(HALF * HALF, LANES)
        near[g] = jnp.transpose(block)[:b_rows]
        return carry

    lax.fori_loop(0, radial_ref.shape[0] // HALF, lay, 0)

    pl.semaphore_wait(barrier, devices - 1)

    def rad_copy(n):
        to = flip(at_b, n, bits_b)
        return pltpu.make_async_remote_copy(
            src_ref=radial_ref.at[pl.ds(to * TILE, TILE)], dst_ref=far.at[at_b],
            send_sem=rad_send, recv_sem=rad_recv, device_id=(at_a, to), device_id_type=MESH,
        )

    pltpu.make_async_copy(radial_ref.at[pl.ds(at_b * TILE, TILE)], far.at[at_b], rad_recv).start()

    def rad_start(n, carry):
        rad_copy(n).start()
        return carry

    lax.fori_loop(1, rb, rad_start, 0)

    def order_of(b):
        i, r = b // per, b % per
        return i * per + (r % 2) * pairs + r // 2

    places = sorted(range(TILE), key=order_of)

    def kick(planes, factor_of, count):
        both = jnp.concatenate(planes, axis=0)
        total = [None, None]
        for k in range(KTERMS):
            applied = jnp.dot(both, weights_ref[k], preferred_element_type=jnp.float32)
            factor = factor_of(k)
            for p in range(2):
                term = applied[p * count:(p + 1) * count] * factor
                total[p] = term if k == 0 else total[p] + term
        return planes[0].astype(jnp.float32) + total[1], planes[1].astype(jnp.float32) - total[0]

    def kick_chunk(q):
        slot = lax.rem(q, 2)
        load(q).wait()

        def group(g, carry):
            count = TILE * TILE
            planes = [stage[slot, p, pl.ds(g * TILE, TILE)].reshape(count, channels) for p in range(2)]
            laid = [near[g * 2 + n, pl.ds(pl.multiple_of(q * TILE, TILE), TILE)] for n in range(2)]

            def factor_of(k):
                return jnp.concatenate([
                    jnp.broadcast_to(laid[n // HALF][:, (n % HALF) * HALF + k:(n % HALF) * HALF + k + 1], (TILE, channels))
                    for n in range(TILE)
                ], axis=0)

            result = kick(planes, factor_of, count)
            for p in range(2):
                turned = jnp.swapaxes(result[p].reshape(TILE, TILE, channels), 0, 1).astype(jnp.bfloat16)
                for row, b in enumerate(places):
                    lower[p, q * TILE + row, g] = turned[b]
            return carry

        lax.fori_loop(0, a_tiles, group, 0)

        @pl.when(q + 2 < chunks)
        def _():
            load(q + 2).start()

    def near_start(q, d):
        for par in range(2):
            to = flip(at_a, d, bits_a)
            source = lower.at[:, pl.ds(q * TILE + to * per + par * pairs, pairs)]
            target = left.at[:, q, :, pl.ds(par * (groups // 2) + at_a * a_tiles, a_tiles)]
            if d == 0:
                pltpu.make_async_copy(source, target, recv_near.at[q]).start()
            else:
                pltpu.make_async_remote_copy(
                    src_ref=source, dst_ref=target, send_sem=send_sem.at[0], recv_sem=recv_near.at[q],
                    device_id=(to, at_b), device_id_type=MESH,
                ).start()

    def home_start(q, d):
        for par in range(2):
            to = flip(at_a, d, bits_a)
            source = right.at[:, q, :, pl.ds(par * (groups // 2) + to * a_tiles, a_tiles)]
            target = upper.at[:, pl.ds(q * TILE + at_a * per + par * pairs, pairs)]
            if d == 0:
                pltpu.make_async_copy(source, target, recv_home.at[q]).start()
            else:
                pltpu.make_async_remote_copy(
                    src_ref=source, dst_ref=target, send_sem=send_sem.at[3], recv_sem=recv_home.at[q],
                    device_id=(to, at_b), device_id_type=MESH,
                ).start()

    near_order = list(range(ra // 2, ra)) + list(range(1, ra // 2)) + [0]

    def far_start(q, h):
        def place(i, j):
            return (i * rb + j) * 2 + h

        row = h * halfway + at_b * chunks + q

        def one(d, carry):
            to_a, to_b = partner(d)
            pltpu.make_async_remote_copy(
                src_ref=right.at[:, q, :, place(to_a, to_b)], dst_ref=upper.at[:, row, pl.ds(at_a * pairs, pairs)],
                send_sem=send_sem.at[1], recv_sem=recv_far.at[h], device_id=(to_a, to_b), device_id_type=MESH,
            ).start()
            return carry

        lax.fori_loop(1, devices, one, 0)
        pltpu.make_async_copy(
            right.at[:, q, :, place(at_a, at_b)], upper.at[:, row, pl.ds(at_a * pairs, pairs)], recv_far.at[h]
        ).start()

    def back_start(q, h):
        place = (at_a * rb + at_b) * 2 + h

        def one(d, carry):
            to_a, to_b = partner(d)
            pltpu.make_async_remote_copy(
                src_ref=lower.at[:, h * halfway + to_b * chunks + q, pl.ds(to_a * pairs, pairs)],
                dst_ref=left.at[:, q, :, place],
                send_sem=send_sem.at[2], recv_sem=recv_back.at[q], device_id=(to_a, to_b), device_id_type=MESH,
            ).start()
            return carry

        lax.fori_loop(1, devices, one, 0)
        pltpu.make_async_copy(
            lower.at[:, h * halfway + at_b * chunks + q, pl.ds(at_a * pairs, pairs)], left.at[:, q, :, place],
            recv_back.at[q],
        ).start()

    def arrived(ref, sem):
        pltpu.make_async_copy(ref, ref, sem).wait()

    def first_chunk(q):
        arrived(left.at[:, q], recv_near.at[q])

        def pair(bp, carry):
            made = []
            for par in range(2):
                span = pl.ds(par * (groups // 2), groups // 2)
                both = jnp.concatenate([left[p, q, bp, span].reshape(depth, channels) for p in range(2)], axis=0)
                made.append(jnp.dot(first_mat[...], both, preferred_element_type=jnp.float32))
            for p in range(2):
                parts = [m[p * depth:(p + 1) * depth].reshape(groups, HALF, channels) for m in made]
                right[p, q, bp] = jnp.concatenate(parts, axis=1).astype(jnp.bfloat16)
            return carry

        lax.fori_loop(0, pairs, pair, 0)

    def last_chunk(q):
        arrived(left.at[:, q], recv_back.at[q])

        def pair(bp, carry):
            wide = [left[p, q, bp].astype(jnp.float32) for p in range(2)]
            for par in range(2):
                both = jnp.concatenate([
                    w[:, par * HALF:(par + 1) * HALF].reshape(depth, channels).astype(jnp.bfloat16) for w in wide
                ], axis=0)
                made = jnp.dot(first_mat[...], both, preferred_element_type=jnp.float32)
                for p in range(2):
                    right[p, q, bp, pl.ds(par * (groups // 2), groups // 2)] = made[
                        p * depth:(p + 1) * depth].reshape(groups // 2, TILE, channels).astype(jnp.bfloat16)
            return carry

        lax.fori_loop(0, pairs, pair, 0)

    def finish_chunk(q):
        slot = lax.rem(q, 2)
        arrived(upper.at[:, pl.ds(q * TILE, TILE)], recv_home.at[q])

        @pl.when(q >= 2)
        def _():
            store(q - 2).wait()

        def group(g, carry):
            for p in range(2):
                rows = [None] * TILE
                for row, b in enumerate(places):
                    rows[b] = upper[p, q * TILE + row, g].astype(jnp.float32)
                turned = jnp.swapaxes(jnp.stack(rows), 0, 1)
                stage[slot, p, pl.ds(g * TILE, TILE)] = turned.astype(jnp.bfloat16)
            return carry

        lax.fori_loop(0, a_tiles, group, 0)
        store(q).start()

    def opening(t, carry):
        @pl.when(t < chunks)
        def _():
            kick_chunk(t)
            for d in near_order:
                near_start(t, d)

        @pl.when(t >= 2)
        def _():
            q = t - 2
            first_chunk(q)
            far_start(q, 0)

            @pl.when(q < chunks // 2)
            def _():
                far_start(q, 1)

            @pl.when(q == chunks - 1)
            def _():
                def rest(n, carry):
                    far_start(n, 1)
                    return carry

                lax.fori_loop(chunks // 2, chunks, rest, 0)

        return carry

    lax.fori_loop(0, chunks + 2, opening, 0)

    arrived(lower.at[:, 0:lower.shape[1] * (ra - 1) // ra], send_sem.at[0])
    arrived(far, rad_recv)

    width = LANES * 1
    sheets = channels // width
    block = a_tiles * TILE

    def middle(h, carry):
        arrived(upper.at[:, pl.ds(h * halfway, halfway)], recv_far.at[h])

        def spread(m, carry):
            for p in range(2):
                wide = upper[p, h * halfway + m].astype(jnp.float32).reshape(block, channels)
                for s in range(sheets):
                    turn[p, s, pl.ds(pl.multiple_of(m * block, block), block)] = wide[:, s * width:(s + 1) * width]
            return carry

        lax.fori_loop(0, halfway, spread, 0)

        def line(a, carry):
            size = second_ref.shape[1]
            at = pl.ds(a, size, stride=HALF)
            both = jnp.concatenate([
                jnp.concatenate([turn[p, s, at] for s in range(sheets)], axis=1).astype(jnp.bfloat16) for p in range(2)
            ], axis=0)
            made = jnp.dot(second_mat[...], both, preferred_element_type=jnp.float32).astype(jnp.bfloat16)
            laid = jnp.transpose(far[:, h * HALF + a].reshape(rb * HALF, LANES))[:b_rows]

            def factor_of(k):
                return jnp.concatenate([
                    jnp.broadcast_to(laid[:, n * HALF + k:n * HALF + k + 1], (b_rows, channels)) for n in range(rb)
                ], axis=0)

            kicked = kick([made[:size], made[size:]], factor_of, size)
            both = jnp.concatenate([x.astype(jnp.bfloat16) for x in kicked], axis=0)
            made = jnp.dot(second_mat[...], both, preferred_element_type=jnp.float32)
            for p in range(2):
                for s in range(sheets):
                    turn[p, s, at] = made[p * size:(p + 1) * size, s * width:(s + 1) * width]
            return carry

        lax.fori_loop(0, HALF, line, 0)

        def gather(m, carry):
            for p in range(2):
                wide = jnp.concatenate([
                    turn[p, s, pl.ds(pl.multiple_of(m * block, block), block)] for s in range(sheets)
                ], axis=1)
                lower[p, h * halfway + m] = wide.astype(jnp.bfloat16).reshape(a_tiles, TILE, channels)
            return carry

        lax.fori_loop(0, halfway, gather, 0)

        @pl.when(h == 0)
        def _():
            def early(q, carry):
                back_start(q, 0)
                return carry

            lax.fori_loop(0, chunks // 2, early, 0)

        @pl.when(h == 1)
        def _():
            def late(q, carry):
                @pl.when(q >= chunks // 2)
                def _():
                    back_start(q, 0)

                back_start(q, 1)
                return carry

            lax.fori_loop(0, chunks, late, 0)

        return carry

    lax.fori_loop(0, 2, middle, 0)

    arrived(right.at[:, :, :, 0:groups * (devices - 1) // devices], send_sem.at[1])

    def closing(t, carry):
        @pl.when(t < chunks)
        def _():
            last_chunk(t)
            for d in near_order:
                home_start(t, d)

        @pl.when(t >= 1)
        def _():
            finish_chunk(t - 1)

        return carry

    lax.fori_loop(0, chunks + 1, closing, 0)

    store(jnp.int32(chunks - 2)).wait()
    store(jnp.int32(chunks - 1)).wait()
    arrived(lower.at[:, 0:lower.shape[1] * (devices - 1) // devices], send_sem.at[2])
    arrived(right.at[:, :, :, 0:groups * (ra - 1) // ra], send_sem.at[3])
    arrived(far.at[0:rb - 1], rad_send)


def on_device(amplitude, coupling, pattern, radial, first_prop, second_prop):
    a_rows, b_rows, channels = amplitude.shape[1:]
    n_a, n_b = first_prop.shape[1], second_prop.shape[1]
    ra, rb = lax.axis_size("ra"), lax.axis_size("rb")
    devices = ra * rb
    chunks = b_rows // TILE
    fits = (
        channels == 2 * LANES and ra & (ra - 1) == 0 and rb == HALF and ra in (2, 4) and n_a == n_b
        and n_a == TILE * devices and n_b == TILE * devices and a_rows % TILE == 0 and b_rows % TILE == 0
        and chunks % 2 == 0 and chunks == ra and a_rows == TILE * HALF and b_rows <= LANES
    )
    if not fits:
        return plain(amplitude, coupling, pattern, radial, first_prop, second_prop)

    pairs = TILE // ra // 2
    groups = n_a // HALF
    weights = masked_weights(coupling, pattern).transpose(0, 2, 1)
    laid = jnp.pad(radial.transpose(1, 0, 2), ((0, 0), (0, HALF - KTERMS), (0, LANES - b_rows)))
    flat = (2, chunks * TILE, a_rows // TILE, TILE, channels)
    tall = (2, chunks, pairs, groups, TILE, channels)
    whole = pl.BlockSpec(memory_space=pltpu.VMEM)
    kept = pl.BlockSpec(memory_space=pl.ANY)
    dma = pltpu.SemaphoreType.DMA
    return pl.pallas_call(
        functools.partial(fused_kernel, ra, rb),
        in_specs=[kept, whole, whole, whole, whole],
        out_specs=kept,
        out_shape=jax.ShapeDtypeStruct(amplitude.shape, jnp.bfloat16),
        scratch_shapes=[
            pltpu.VMEM(flat, jnp.bfloat16),
            pltpu.VMEM(flat, jnp.bfloat16),
            pltpu.VMEM(tall, jnp.bfloat16),
            pltpu.VMEM(tall, jnp.bfloat16),
            pltpu.VMEM((2, channels // LANES, n_b * HALF, LANES), jnp.float32),
            pltpu.VMEM((2, 2, a_rows, TILE, channels), jnp.bfloat16),
            pltpu.VMEM((2 * n_a, 2 * n_a), jnp.bfloat16),
            pltpu.VMEM((2 * n_b, 2 * n_b), jnp.bfloat16),
            pltpu.VMEM((a_rows // HALF, b_rows, HALF * HALF), jnp.float32),
            pltpu.VMEM((rb, TILE, HALF, LANES), jnp.float32),
            dma((2,)), dma((2,)), dma((4,)), dma((chunks,)), dma((2,)), dma((chunks,)), dma((chunks,)),
            dma(()), dma(()),
        ],
        compiler_params=pltpu.CompilerParams(
            collective_id=0, has_side_effects=True, vmem_limit_bytes=63 * 2**20
        ),
    )(amplitude, weights, laid, first_prop, second_prop)


def solution(mesh):
    return jax.shard_map(
        on_device,
        mesh=mesh,
        in_specs=(P(None, "ra", "rb", None), P(), P(), P(None, "ra", "rb"), P(), P()),
        out_specs=P(None, "ra", "rb", None),
        check_vma=False,
    )
```

```python
import functools

import jax
import jax.numpy as jnp
from jax import lax
from jax.experimental import pallas as pl
from jax.experimental.pallas import tpu as pltpu
from jax.sharding import PartitionSpec as P

KTERMS = 6
STEPS = 2
LANES = 128
TILE = 16
HALF = 8
MESH = pl.DeviceIdType.MESH


def complex_rows(matrix, piece):
    form = "ac,cqw->aqw"
    real_part = jnp.einsum(
        form, matrix[0], piece[0], preferred_element_type=jnp.float32
    ) - jnp.einsum(form, matrix[1], piece[1], preferred_element_type=jnp.float32)
    imag_part = jnp.einsum(
        form, matrix[0], piece[1], preferred_element_type=jnp.float32
    ) + jnp.einsum(form, matrix[1], piece[0], preferred_element_type=jnp.float32)
    return jnp.stack([real_part, imag_part]).astype(jnp.bfloat16)


def masked_weights(coupling, pattern):
    channels = coupling.shape[1]
    count = pattern.shape[1]
    block_size = channels // count
    spread = jnp.broadcast_to(
        pattern[:, :, None, :, None], (KTERMS, count, block_size, count, block_size)
    )
    return coupling * spread.reshape(KTERMS, channels, channels).astype(jnp.bfloat16)


def plain(amplitude, coupling, pattern, radial, first_prop, second_prop):
    first_rows, second_rows, channels = (amplitude.shape[1], amplitude.shape[2], amplitude.shape[3])
    cells = first_rows * second_rows
    groups_a = lax.axis_size("ra")
    groups_b = lax.axis_size("rb")
    width_a = channels // groups_a
    width_b = channels // groups_b
    weights = masked_weights(coupling, pattern)
    radial_cells = radial.reshape(KTERMS, cells).T
    for sweep in range(STEPS):
        flat = amplitude.reshape(2 * cells, channels)
        applied = jnp.einsum("mj,kij->mki", flat, weights, preferred_element_type=jnp.float32)
        applied = applied.reshape(2, cells, KTERMS, channels)
        coupled = jnp.sum(applied * radial_cells[None, :, :, None], axis=2)
        wide = amplitude.reshape(2, cells, channels).astype(jnp.float32)
        kicked = jnp.stack([wide[0] + coupled[1], wide[1] - coupled[0]]).astype(jnp.bfloat16)
        grouped = kicked.reshape(2, first_rows, second_rows, groups_a, width_a)
        grouped = grouped.transpose(0, 1, 3, 2, 4).reshape(
            2, first_rows, groups_a, second_rows * width_a
        )
        half = complex_rows(
            first_prop, lax.all_to_all(grouped, "ra", split_axis=2, concat_axis=1, tiled=True)
        )
        restored = lax.all_to_all(half, "ra", split_axis=1, concat_axis=2, tiled=True)
        restored = restored.reshape(2, first_rows, groups_a, second_rows, width_a)
        restored = restored.transpose(0, 1, 3, 2, 4).reshape(
            2, first_rows, second_rows, groups_b, width_b
        )
        regrouped = restored.transpose(0, 2, 3, 1, 4).reshape(
            2, second_rows, groups_b, first_rows * width_b
        )
        moved = complex_rows(
            second_prop, lax.all_to_all(regrouped, "rb", split_axis=2, concat_axis=1, tiled=True)
        )
        settled = lax.all_to_all(moved, "rb", split_axis=1, concat_axis=2, tiled=True)
        settled = settled.reshape(2, second_rows, groups_b, first_rows, width_b)
        amplitude = settled.transpose(0, 3, 1, 2, 4).reshape(2, first_rows, second_rows, channels)
    return amplitude


def flip(value, mask, bits):
    out = 0
    for n in range(bits):
        weight = 1 << n
        out = out + lax.rem(lax.div(value, weight) + lax.div(mask, weight), 2) * weight
    return out


def fused_kernel(ra, rb, amp_ref, coupling_ref, pattern_ref, radial_ref, first_ref, second_ref, out_ref,
                 lower, upper, left, right, turn, stage, first_mat, second_mat, weights_ref, near, far, lines,
                 load_sem, store_sem, send_sem, recv_near, recv_far, recv_back, recv_home, rad_send, rad_recv):
    at_a, at_b = lax.axis_index("ra"), lax.axis_index("rb")
    bits_a, bits_b = ra.bit_length() - 1, rb.bit_length() - 1
    chunks = left.shape[1]
    pairs = left.shape[2]
    sixteens = left.shape[4]
    groups = 2 * sixteens
    per = pairs * 2
    depth = first_ref.shape[1]
    halfway = lower.shape[1] // 2
    channels = lower.shape[4]
    a_tiles = lower.shape[2]
    devices = ra * rb
    route = [("b", bits_b - 1)] + [("b", n) for n in range(bits_b - 1)]
    route = route + [("a", n) for n in range(bits_a)]

    def partner(d):
        mask_a, mask_b = 0, 0
        for n, (axis, bit) in enumerate(route):
            one = lax.rem(lax.div(d, 1 << n), 2) * (1 << bit)
            if axis == "a":
                mask_a = mask_a + one
            else:
                mask_b = mask_b + one
        return flip(at_a, mask_a, bits_a), flip(at_b, mask_b, bits_b)

    barrier = pltpu.get_barrier_semaphore()

    def greet(d, carry):
        to_a, to_b = partner(d)
        pl.semaphore_signal(barrier, inc=1, device_id=(to_a, to_b), device_id_type=MESH)
        return carry

    lax.fori_loop(1, devices, greet, 0)

    def load(q):
        slot = lax.rem(q, 2)
        return pltpu.make_async_copy(amp_ref.at[:, :, pl.ds(q * TILE, TILE)], stage.at[slot], load_sem.at[slot])

    def store(q):
        slot = lax.rem(q, 2)
        return pltpu.make_async_copy(stage.at[slot], out_ref.at[:, :, pl.ds(q * TILE, TILE)], store_sem.at[slot])

    load(jnp.int32(0)).start()
    load(jnp.int32(1)).start()

    for source, target in ((first_ref, first_mat), (second_ref, second_mat)):
        target[:depth, :depth] = source[0]
        target[depth:, depth:] = source[0]
        target[:depth, depth:] = -source[1]
        target[depth:, :depth] = source[1]

    b_rows = amp_ref.shape[2]
    blocks = pattern_ref.shape[1]
    size_block = channels // blocks
    lane = lax.broadcasted_iota(jnp.int32, (size_block, channels), 1)
    for k in range(KTERMS):
        masked = []
        for i in range(blocks):
            keep = jnp.zeros((size_block, channels), jnp.float32)
            for j in range(blocks):
                inside = (lane >= j * size_block) & (lane < (j + 1) * size_block)
                keep = jnp.where(inside, pattern_ref[k, i, j].astype(jnp.float32), keep)
            masked.append(coupling_ref[k, i * size_block:(i + 1) * size_block].astype(jnp.float32) * keep)
        weights_ref[k] = jnp.transpose(jnp.concatenate(masked, axis=0)).astype(jnp.bfloat16)

    def lay(g, carry):
        at = pl.ds(pl.multiple_of(g * HALF, HALF), HALF)
        near[g] = jnp.transpose(radial_ref[:, at].reshape(KTERMS * HALF, b_rows))
        return carry

    lax.fori_loop(0, radial_ref.shape[1] // HALF, lay, 0)

    pl.semaphore_wait(barrier, devices - 1)

    def rad_copy(n):
        to = flip(at_b, n, bits_b)
        return pltpu.make_async_remote_copy(
            src_ref=radial_ref.at[:, pl.ds(pl.multiple_of(to * TILE, TILE), TILE)], dst_ref=far.at[at_b],
            send_sem=rad_send, recv_sem=rad_recv, device_id=(at_a, to), device_id_type=MESH,
        )

    pltpu.make_async_copy(
        radial_ref.at[:, pl.ds(pl.multiple_of(at_b * TILE, TILE), TILE)], far.at[at_b], rad_recv
    ).start()

    def rad_start(n, carry):
        rad_copy(n).start()
        return carry

    lax.fori_loop(1, rb, rad_start, 0)

    def kick(planes, factor_of, count):
        both = jnp.concatenate(planes, axis=0)
        total = [None, None]
        for k in range(KTERMS):
            applied = jnp.dot(both, weights_ref[k], preferred_element_type=jnp.float32)
            factor = factor_of(k)
            for p in range(2):
                term = applied[p * count:(p + 1) * count] * factor
                total[p] = term if k == 0 else total[p] + term
        return planes[0].astype(jnp.float32) + total[1], planes[1].astype(jnp.float32) - total[0]

    def kick_chunk(q):
        slot = lax.rem(q, 2)
        load(q).wait()

        def group(g, carry):
            count = TILE * TILE
            planes = [stage[slot, p, pl.ds(g * TILE, TILE)].reshape(count, channels) for p in range(2)]
            laid = [near[g * 2 + n, pl.ds(pl.multiple_of(q * TILE, TILE), TILE)] for n in range(2)]

            def factor_of(k):
                return jnp.concatenate([
                    jnp.broadcast_to(laid[n // HALF][:, k * HALF + n % HALF:k * HALF + n % HALF + 1], (TILE, channels))
                    for n in range(TILE)
                ], axis=0)

            result = kick(planes, factor_of, count)
            for p in range(2):
                turned = jnp.swapaxes(result[p].reshape(TILE, TILE, channels), 0, 1).astype(jnp.bfloat16)
                lower[p, pl.ds(q * TILE, TILE), g] = turned
            return carry

        lax.fori_loop(0, a_tiles, group, 0)

        @pl.when(q + 2 < chunks)
        def _():
            load(q + 2).start()

    def near_start(q, bp, d):
        to = flip(at_a, d, bits_a)
        source = lower.at[:, pl.ds(q * TILE + to * per + bp * 2, 2)]
        target = left.at[:, q, bp, :, pl.ds(at_a * a_tiles, a_tiles)]
        sem = recv_near.at[q * pairs + bp]
        if d == 0:
            pltpu.make_async_copy(source, target, sem).start()
        else:
            pltpu.make_async_remote_copy(
                src_ref=source, dst_ref=target, send_sem=send_sem.at[0], recv_sem=sem,
                device_id=(to, at_b), device_id_type=MESH,
            ).start()

    def home_start(q, bp, d):
        to = flip(at_a, d, bits_a)
        source = right.at[:, q, bp, :, pl.ds(to * a_tiles, a_tiles)]
        target = upper.at[:, pl.ds(q * TILE + at_a * per + bp * 2, 2)]
        if d == 0:
            pltpu.make_async_copy(source, target, recv_home.at[q]).start()
        else:
            pltpu.make_async_remote_copy(
                src_ref=source, dst_ref=target, send_sem=send_sem.at[3], recv_sem=recv_home.at[q],
                device_id=(to, at_b), device_id_type=MESH,
            ).start()

    near_order = list(range(ra // 2, ra)) + list(range(1, ra // 2)) + [0]
    side = devices // 2

    def place(i, j, h):
        index = (i * rb + j) * 2 + h
        return lax.div(index, sixteens), lax.rem(index, sixteens)

    def far_start(c, h, crossing):
        q, bp = lax.div(c, pairs), lax.rem(c, pairs)
        row = h * halfway + at_b * chunks + q
        target = upper.at[:, row, at_a * pairs + bp]

        def one(d, carry):
            to_a, to_b = partner(d)
            high, low = place(to_a, to_b, h)
            pltpu.make_async_remote_copy(
                src_ref=right.at[:, q, bp, high, low], dst_ref=target,
                send_sem=send_sem.at[1], recv_sem=recv_far.at[h], device_id=(to_a, to_b), device_id_type=MESH,
            ).start()
            return carry

        if crossing:
            lax.fori_loop(side, devices, one, 0)
        else:
            lax.fori_loop(1, side, one, 0)
            high, low = place(at_a, at_b, h)
            pltpu.make_async_copy(right.at[:, q, bp, high, low], target, recv_far.at[h]).start()

    def back_start(c, h, crossing):
        q, bp = lax.div(c, pairs), lax.rem(c, pairs)
        high, low = place(at_a, at_b, h)
        target = left.at[:, q, bp, high, low]

        def one(d, carry):
            to_a, to_b = partner(d)
            pltpu.make_async_remote_copy(
                src_ref=lower.at[:, h * halfway + to_b * chunks + q, to_a * pairs + bp], dst_ref=target,
                send_sem=send_sem.at[2], recv_sem=recv_back.at[c], device_id=(to_a, to_b), device_id_type=MESH,
            ).start()
            return carry

        if crossing:
            lax.fori_loop(side, devices, one, 0)
        else:
            lax.fori_loop(1, side, one, 0)
            pltpu.make_async_copy(
                lower.at[:, h * halfway + at_b * chunks + q, at_a * pairs + bp], target, recv_back.at[c]
            ).start()

    def every(action):
        def one(c, carry):
            action(c)
            return carry

        lax.fori_loop(0, chunks * pairs, one, 0)

    def arrived(ref, sem):
        pltpu.make_async_copy(ref, ref, sem).wait()

    def first_chunk(c):
        q, bp = lax.div(c, pairs), lax.rem(c, pairs)
        arrived(left.at[:, q, bp], recv_near.at[c])
        made = []
        for par in range(2):
            both = jnp.concatenate([left[p, q, bp, par].reshape(depth, channels) for p in range(2)], axis=0)
            made.append(jnp.dot(first_mat[...], both, preferred_element_type=jnp.float32))
        for p in range(2):
            parts = [m[p * depth:(p + 1) * depth].reshape(groups, HALF, channels) for m in made]
            mixed = jnp.concatenate(parts, axis=1).astype(jnp.bfloat16)
            right[p, q, bp] = mixed.reshape(2, sixteens, TILE, channels)

    def last_chunk(c):
        q, bp = lax.div(c, pairs), lax.rem(c, pairs)
        arrived(left.at[:, q, bp], recv_back.at[c])
        wide = [left[p, q, bp].reshape(groups, TILE, channels).astype(jnp.float32) for p in range(2)]
        for par in range(2):
            both = jnp.concatenate([
                w[:, par * HALF:(par + 1) * HALF].reshape(depth, channels).astype(jnp.bfloat16) for w in wide
            ], axis=0)
            made = jnp.dot(first_mat[...], both, preferred_element_type=jnp.float32)
            for p in range(2):
                part = made[p * depth:(p + 1) * depth].reshape(sixteens, TILE, channels)
                right[p, q, bp, par] = part.astype(jnp.bfloat16)

    def finish_chunk(q):
        slot = lax.rem(q, 2)
        arrived(upper.at[:, pl.ds(q * TILE, TILE)], recv_home.at[q])

        @pl.when(q >= 2)
        def _():
            store(q - 2).wait()

        def group(g, carry):
            for p in range(2):
                turned = jnp.swapaxes(upper[p, pl.ds(q * TILE, TILE), g].astype(jnp.float32), 0, 1)
                stage[slot, p, pl.ds(g * TILE, TILE)] = turned.astype(jnp.bfloat16)
            return carry

        lax.fori_loop(0, a_tiles, group, 0)
        store(q).start()

    def opening(t, carry):
        @pl.when(t < chunks)
        def _():
            kick_chunk(t)
            for bp in range(pairs):
                for d in near_order:
                    near_start(t, bp, d)

        @pl.when(t >= 1)
        def _():
            def one(c, carry):
                first_chunk(c)
                far_start(c, 0, False)
                far_start(c, 1, False)
                return carry

            lax.fori_loop((t - 1) * pairs, t * pairs, one, 0)

        return carry

    lax.fori_loop(0, chunks + 1, opening, 0)
    every(lambda c: far_start(c, 0, True))
    every(lambda c: far_start(c, 1, True))

    arrived(lower.at[:, 0:lower.shape[1] * (ra - 1) // ra], send_sem.at[0])
    arrived(far, rad_recv)

    width = LANES * 1
    sheets = channels // width
    block = a_tiles * TILE

    def middle(h, carry):
        arrived(upper.at[:, pl.ds(h * halfway, halfway)], recv_far.at[h])
        pieces = far[:, :, pl.ds(pl.multiple_of(h * HALF, HALF), HALF)].reshape(rb * KTERMS, HALF, b_rows)
        lines[...] = jnp.swapaxes(pieces, 0, 1)

        def spread(m, carry):
            for p in range(2):
                wide = upper[p, h * halfway + m].astype(jnp.float32).reshape(block, channels)
                for s in range(sheets):
                    turn[p, s, pl.ds(pl.multiple_of(m * block, block), block)] = wide[:, s * width:(s + 1) * width]
            return carry

        lax.fori_loop(0, halfway, spread, 0)

        def line(a, carry):
            size = second_ref.shape[1]
            at = pl.ds(a, size, stride=HALF)
            both = jnp.concatenate([
                jnp.concatenate([turn[p, s, at] for s in range(sheets)], axis=1).astype(jnp.bfloat16) for p in range(2)
            ], axis=0)
            made = jnp.dot(second_mat[...], both, preferred_element_type=jnp.float32).astype(jnp.bfloat16)
            laid = jnp.transpose(lines[a])

            def factor_of(k):
                return jnp.concatenate([
                    jnp.broadcast_to(laid[:, n * KTERMS + k:n * KTERMS + k + 1], (b_rows, channels)) for n in range(rb)
                ], axis=0)

            kicked = kick([made[:size], made[size:]], factor_of, size)
            both = jnp.concatenate([x.astype(jnp.bfloat16) for x in kicked], axis=0)
            made = jnp.dot(second_mat[...], both, preferred_element_type=jnp.float32)
            for p in range(2):
                for s in range(sheets):
                    turn[p, s, at] = made[p * size:(p + 1) * size, s * width:(s + 1) * width]
            return carry

        lax.fori_loop(0, HALF, line, 0)

        def gather(m, carry):
            for p in range(2):
                wide = jnp.concatenate([
                    turn[p, s, pl.ds(pl.multiple_of(m * block, block), block)] for s in range(sheets)
                ], axis=1)
                lower[p, h * halfway + m] = wide.astype(jnp.bfloat16).reshape(a_tiles, TILE, channels)
            return carry

        lax.fori_loop(0, halfway, gather, 0)

        every(lambda c: back_start(c, h, True))
        return carry

    lax.fori_loop(0, 2, middle, 0)

    def rest(c):
        back_start(c, 0, False)
        back_start(c, 1, False)

    every(rest)
    arrived(right.at[:, :, :, :, 0:sixteens * (devices - 1) // devices], send_sem.at[1])

    def closing(t, carry):
        @pl.when(t < chunks)
        def _():
            def one(c, carry):
                last_chunk(c)
                for d in near_order:
                    home_start(t, lax.rem(c, pairs), d)
                return carry

            lax.fori_loop(t * pairs, (t + 1) * pairs, one, 0)

        @pl.when(t >= 1)
        def _():
            finish_chunk(t - 1)

        return carry

    lax.fori_loop(0, chunks + 1, closing, 0)

    store(jnp.int32(chunks - 2)).wait()
    store(jnp.int32(chunks - 1)).wait()
    arrived(lower.at[:, 0:lower.shape[1] * (devices - 1) // devices], send_sem.at[2])
    arrived(right.at[:, :, :, :, 0:sixteens * (ra - 1) // ra], send_sem.at[3])
    arrived(far.at[0:rb - 1], rad_send)


def on_device(amplitude, coupling, pattern, radial, first_prop, second_prop):
    a_rows, b_rows, channels = amplitude.shape[1:]
    n_a, n_b = first_prop.shape[1], second_prop.shape[1]
    ra, rb = lax.axis_size("ra"), lax.axis_size("rb")
    devices = ra * rb
    chunks = b_rows // TILE
    fits = (
        channels == 2 * LANES and ra & (ra - 1) == 0 and rb == HALF and ra in (2, 4) and n_a == n_b
        and n_a == TILE * devices and n_b == TILE * devices and a_rows % TILE == 0 and b_rows % TILE == 0
        and chunks % 2 == 0 and chunks == ra and a_rows == TILE * HALF and b_rows <= LANES
    )
    if not fits:
        return plain(amplitude, coupling, pattern, radial, first_prop, second_prop)

    pairs = TILE // ra // 2
    groups = n_a // HALF
    flat = (2, chunks * TILE, a_rows // TILE, TILE, channels)
    tall = (2, chunks, pairs, 2, groups // 2, TILE, channels)
    whole = pl.BlockSpec(memory_space=pltpu.VMEM)
    kept = pl.BlockSpec(memory_space=pl.ANY)
    dma = pltpu.SemaphoreType.DMA
    return pl.pallas_call(
        functools.partial(fused_kernel, ra, rb),
        in_specs=[kept, whole, pl.BlockSpec(memory_space=pltpu.SMEM), whole, whole, whole],
        out_specs=kept,
        out_shape=jax.ShapeDtypeStruct(amplitude.shape, jnp.bfloat16),
        scratch_shapes=[
            pltpu.VMEM(flat, jnp.bfloat16),
            pltpu.VMEM(flat, jnp.bfloat16),
            pltpu.VMEM(tall, jnp.bfloat16),
            pltpu.VMEM(tall, jnp.bfloat16),
            pltpu.VMEM((2, channels // LANES, n_b * HALF, LANES), jnp.float32),
            pltpu.VMEM((2, 2, a_rows, TILE, channels), jnp.bfloat16),
            pltpu.VMEM((2 * n_a, 2 * n_a), jnp.bfloat16),
            pltpu.VMEM((2 * n_b, 2 * n_b), jnp.bfloat16),
            pltpu.VMEM((KTERMS, channels, channels), jnp.bfloat16),
            pltpu.VMEM((a_rows // HALF, b_rows, KTERMS * HALF), jnp.float32),
            pltpu.VMEM((rb, KTERMS, TILE, b_rows), jnp.float32),
            pltpu.VMEM((HALF, rb * KTERMS, b_rows), jnp.float32),
            dma((2,)), dma((2,)), dma((4,)), dma((chunks * pairs,)), dma((2,)), dma((chunks * pairs,)), dma((chunks,)),
            dma(()), dma(()),
        ],
        compiler_params=pltpu.CompilerParams(
            collective_id=0, has_side_effects=True, vmem_limit_bytes=63 * 2**20
        ),
    )(amplitude, coupling, pattern, radial, first_prop, second_prop)


def solution(mesh):
    return jax.shard_map(
        on_device,
        mesh=mesh,
        in_specs=(P(None, "ra", "rb", None), P(), P(), P(None, "ra", "rb"), P(), P()),
        out_specs=P(None, "ra", "rb", None),
        check_vma=False,
    )
```

```python
import functools

import jax
import jax.numpy as jnp
from jax import lax
from jax.experimental import pallas as pl
from jax.experimental.pallas import tpu as pltpu
from jax.sharding import PartitionSpec as P

KTERMS = 6
STEPS = 2
LANES = 128
TILE = 16
HALF = 8
MESH = pl.DeviceIdType.MESH


def complex_rows(matrix, piece):
    form = "ac,cqw->aqw"
    real_part = jnp.einsum(
        form, matrix[0], piece[0], preferred_element_type=jnp.float32
    ) - jnp.einsum(form, matrix[1], piece[1], preferred_element_type=jnp.float32)
    imag_part = jnp.einsum(
        form, matrix[0], piece[1], preferred_element_type=jnp.float32
    ) + jnp.einsum(form, matrix[1], piece[0], preferred_element_type=jnp.float32)
    return jnp.stack([real_part, imag_part]).astype(jnp.bfloat16)


def masked_weights(coupling, pattern):
    channels = coupling.shape[1]
    count = pattern.shape[1]
    block_size = channels // count
    spread = jnp.broadcast_to(
        pattern[:, :, None, :, None], (KTERMS, count, block_size, count, block_size)
    )
    return coupling * spread.reshape(KTERMS, channels, channels).astype(jnp.bfloat16)


def plain(amplitude, coupling, pattern, radial, first_prop, second_prop):
    first_rows, second_rows, channels = (amplitude.shape[1], amplitude.shape[2], amplitude.shape[3])
    cells = first_rows * second_rows
    groups_a = lax.axis_size("ra")
    groups_b = lax.axis_size("rb")
    width_a = channels // groups_a
    width_b = channels // groups_b
    weights = masked_weights(coupling, pattern)
    radial_cells = radial.reshape(KTERMS, cells).T
    for sweep in range(STEPS):
        flat = amplitude.reshape(2 * cells, channels)
        applied = jnp.einsum("mj,kij->mki", flat, weights, preferred_element_type=jnp.float32)
        applied = applied.reshape(2, cells, KTERMS, channels)
        coupled = jnp.sum(applied * radial_cells[None, :, :, None], axis=2)
        wide = amplitude.reshape(2, cells, channels).astype(jnp.float32)
        kicked = jnp.stack([wide[0] + coupled[1], wide[1] - coupled[0]]).astype(jnp.bfloat16)
        grouped = kicked.reshape(2, first_rows, second_rows, groups_a, width_a)
        grouped = grouped.transpose(0, 1, 3, 2, 4).reshape(
            2, first_rows, groups_a, second_rows * width_a
        )
        half = complex_rows(
            first_prop, lax.all_to_all(grouped, "ra", split_axis=2, concat_axis=1, tiled=True)
        )
        restored = lax.all_to_all(half, "ra", split_axis=1, concat_axis=2, tiled=True)
        restored = restored.reshape(2, first_rows, groups_a, second_rows, width_a)
        restored = restored.transpose(0, 1, 3, 2, 4).reshape(
            2, first_rows, second_rows, groups_b, width_b
        )
        regrouped = restored.transpose(0, 2, 3, 1, 4).reshape(
            2, second_rows, groups_b, first_rows * width_b
        )
        moved = complex_rows(
            second_prop, lax.all_to_all(regrouped, "rb", split_axis=2, concat_axis=1, tiled=True)
        )
        settled = lax.all_to_all(moved, "rb", split_axis=1, concat_axis=2, tiled=True)
        settled = settled.reshape(2, second_rows, groups_b, first_rows, width_b)
        amplitude = settled.transpose(0, 3, 1, 2, 4).reshape(2, first_rows, second_rows, channels)
    return amplitude


BACK_LEAD = 2
FAR_LEAD = 2


def flip(value, mask, bits):
    out = 0
    for n in range(bits):
        weight = 1 << n
        out = out + lax.rem(lax.div(value, weight) + lax.div(mask, weight), 2) * weight
    return out


def fused_kernel(ra, rb, amp_ref, coupling_ref, pattern_ref, turned_ref, first_ref, second_ref, out_ref,
                 lower, upper, left, right, turn, stage, first_mat, second_mat, weights_ref, radial_ref, near, far, lines,
                 load_sem, store_sem, send_sem, recv_near, recv_far, recv_back, recv_home, rad_send, rad_recv):
    at_a, at_b = lax.axis_index("ra"), lax.axis_index("rb")
    bits_a, bits_b = ra.bit_length() - 1, rb.bit_length() - 1
    chunks = left.shape[1]
    pairs = left.shape[2]
    sixteens = left.shape[4]
    groups = 2 * sixteens
    per = pairs * 2
    depth = first_ref.shape[1]
    halfway = lower.shape[1] // 2
    channels = lower.shape[4]
    a_tiles = lower.shape[2]
    devices = ra * rb
    route = [("b", bits_b - 1)] + [("b", n) for n in range(bits_b - 1)]
    route = route + [("a", n) for n in range(bits_a)]

    def partner(d):
        mask_a, mask_b = 0, 0
        for n, (axis, bit) in enumerate(route):
            one = lax.rem(lax.div(d, 1 << n), 2) * (1 << bit)
            if axis == "a":
                mask_a = mask_a + one
            else:
                mask_b = mask_b + one
        return flip(at_a, mask_a, bits_a), flip(at_b, mask_b, bits_b)

    barrier = pltpu.get_barrier_semaphore()

    def greet(d, carry):
        to_a, to_b = partner(d)
        pl.semaphore_signal(barrier, inc=1, device_id=(to_a, to_b), device_id_type=MESH)
        return carry

    lax.fori_loop(1, devices, greet, 0)

    def load(q):
        slot = lax.rem(q, 2)
        return pltpu.make_async_copy(amp_ref.at[:, :, pl.ds(q * TILE, TILE)], stage.at[slot], load_sem.at[slot])

    def store(q):
        tile = pl.ds(q * TILE, TILE)
        return pltpu.make_async_copy(upper.at[:, tile], out_ref.at[:, tile], store_sem)

    load(jnp.int32(0)).start()
    load(jnp.int32(1)).start()

    b_rows = amp_ref.shape[2]
    blocks = pattern_ref.shape[0]
    size_block = channels // blocks
    lane = lax.broadcasted_iota(jnp.int32, (size_block, channels), 1)
    for k in range(KTERMS):
        masked = []
        for i in range(blocks):
            keep = jnp.zeros((size_block, channels), jnp.float32)
            for j in range(blocks):
                inside = (lane >= j * size_block) & (lane < (j + 1) * size_block)
                keep = jnp.where(inside, pattern_ref[i, j, k].astype(jnp.float32), keep)
            masked.append(coupling_ref[k, i * size_block:(i + 1) * size_block].astype(jnp.float32) * keep)
        weights_ref[k] = jnp.transpose(jnp.concatenate(masked, axis=0)).astype(jnp.bfloat16)

    for k in range(KTERMS):
        radial_ref[k] = jnp.transpose(turned_ref[k])

    def lay(g, carry):
        at = pl.ds(pl.multiple_of(g * HALF, HALF), HALF)
        near[g] = jnp.transpose(radial_ref[:, at].reshape(KTERMS * HALF, b_rows))
        return carry

    lax.fori_loop(0, radial_ref.shape[1] // HALF, lay, 0)

    def kick(planes, factor_of, count):
        both = jnp.concatenate(planes, axis=0)
        total = [None, None]
        for k in range(KTERMS):
            applied = jnp.dot(both, weights_ref[k], preferred_element_type=jnp.float32)
            factor = factor_of(k)
            for p in range(2):
                term = applied[p * count:(p + 1) * count] * factor
                total[p] = term if k == 0 else total[p] + term
        return planes[0].astype(jnp.float32) + total[1], planes[1].astype(jnp.float32) - total[0]

    def kick_chunk(q):
        slot = lax.rem(q, 2)
        load(q).wait()

        def group(g, carry):
            count = TILE * TILE
            planes = [stage[slot, p, pl.ds(g * TILE, TILE)].reshape(count, channels) for p in range(2)]
            laid = [near[g * 2 + n, pl.ds(pl.multiple_of(q * TILE, TILE), TILE)] for n in range(2)]

            def factor_of(k):
                return jnp.concatenate([
                    jnp.broadcast_to(laid[n // HALF][:, k * HALF + n % HALF:k * HALF + n % HALF + 1], (TILE, channels))
                    for n in range(TILE)
                ], axis=0)

            result = kick(planes, factor_of, count)
            for p in range(2):
                turned = jnp.swapaxes(result[p].reshape(TILE, TILE, channels), 0, 1).astype(jnp.bfloat16)
                lower[p, pl.ds(q * TILE, TILE), g] = turned
            return carry

        lax.fori_loop(0, a_tiles, group, 0)

        @pl.when(q + 2 < chunks)
        def _():
            load(q + 2).start()

    def near_start(q, bp, d):
        to = flip(at_a, d, bits_a)
        source = lower.at[:, pl.ds(q * TILE + to * per + bp * 2, 2)]
        target = left.at[:, q, bp, :, pl.ds(at_a * a_tiles, a_tiles)]
        sem = recv_near.at[q * pairs + bp]
        if d == 0:
            pltpu.make_async_copy(source, target, sem).start()
        else:
            pltpu.make_async_remote_copy(
                src_ref=source, dst_ref=target, send_sem=send_sem.at[0], recv_sem=sem,
                device_id=(to, at_b), device_id_type=MESH,
            ).start()

    def home_start(q, bp, d):
        to = flip(at_a, d, bits_a)
        source = right.at[:, q, bp, :, pl.ds(to * a_tiles, a_tiles)]
        target = upper.at[:, pl.ds(q * TILE + at_a * per + bp * 2, 2)]
        if d == 0:
            pltpu.make_async_copy(source, target, recv_home.at[q]).start()
        else:
            pltpu.make_async_remote_copy(
                src_ref=source, dst_ref=target, send_sem=send_sem.at[3], recv_sem=recv_home.at[q],
                device_id=(to, at_b), device_id_type=MESH,
            ).start()

    near_order = list(range(ra // 2, ra)) + list(range(1, ra // 2)) + [0]
    side = devices // 2

    def place(i, j, h):
        index = (i * rb + j) * 2 + h
        return lax.div(index, sixteens), lax.rem(index, sixteens)

    def far_start(c, h, crossing):
        q, bp = lax.div(c, pairs), lax.rem(c, pairs)
        row = h * halfway + at_b * chunks + q
        target = upper.at[:, row, at_a * pairs + bp]

        def one(d, carry):
            to_a, to_b = partner(d)
            high, low = place(to_a, to_b, h)
            pltpu.make_async_remote_copy(
                src_ref=right.at[:, q, bp, high, low], dst_ref=target,
                send_sem=send_sem.at[1], recv_sem=recv_far.at[h], device_id=(to_a, to_b), device_id_type=MESH,
            ).start()
            return carry

        if crossing:
            lax.fori_loop(side, devices, one, 0)
        else:
            lax.fori_loop(1, side, one, 0)
            high, low = place(at_a, at_b, h)
            pltpu.make_async_copy(right.at[:, q, bp, high, low], target, recv_far.at[h]).start()

    def back_start(c, h, crossing):
        q, bp = lax.div(c, pairs), lax.rem(c, pairs)
        high, low = place(at_a, at_b, h)
        target = left.at[:, q, bp, high, low]

        def one(d, carry):
            to_a, to_b = partner(d)
            pltpu.make_async_remote_copy(
                src_ref=lower.at[:, h * halfway + to_b * chunks + q, to_a * pairs + bp], dst_ref=target,
                send_sem=send_sem.at[2], recv_sem=recv_back.at[c], device_id=(to_a, to_b), device_id_type=MESH,
            ).start()
            return carry

        if crossing:
            lax.fori_loop(side, devices, one, 0)
        else:
            lax.fori_loop(1, side, one, 0)
            pltpu.make_async_copy(
                lower.at[:, h * halfway + at_b * chunks + q, at_a * pairs + bp], target, recv_back.at[c]
            ).start()

    def every(action):
        def one(c, carry):
            action(c)
            return carry

        lax.fori_loop(0, chunks * pairs, one, 0)

    def arrived(ref, sem):
        pltpu.make_async_copy(ref, ref, sem).wait()

    def first_chunk(c):
        q, bp = lax.div(c, pairs), lax.rem(c, pairs)
        arrived(left.at[:, q, bp], recv_near.at[c])
        made = []
        for par in range(2):
            both = jnp.concatenate([left[p, q, bp, par].reshape(depth, channels) for p in range(2)], axis=0)
            made.append(jnp.dot(first_mat[...], both, preferred_element_type=jnp.float32))
        for p in range(2):
            parts = [m[p * depth:(p + 1) * depth].reshape(groups, HALF, channels) for m in made]
            mixed = jnp.concatenate(parts, axis=1).astype(jnp.bfloat16)
            right[p, q, bp] = mixed.reshape(2, sixteens, TILE, channels)

    def last_chunk(c):
        q, bp = lax.div(c, pairs), lax.rem(c, pairs)
        arrived(left.at[:, q, bp], recv_back.at[c])
        wide = [left[p, q, bp].reshape(groups, TILE, channels).astype(jnp.float32) for p in range(2)]
        for par in range(2):
            both = jnp.concatenate([
                w[:, par * HALF:(par + 1) * HALF].reshape(depth, channels).astype(jnp.bfloat16) for w in wide
            ], axis=0)
            made = jnp.dot(first_mat[...], both, preferred_element_type=jnp.float32)
            for p in range(2):
                part = made[p * depth:(p + 1) * depth].reshape(sixteens, TILE, channels)
                right[p, q, bp, par] = part.astype(jnp.bfloat16)

    def finish_chunk(q):
        arrived(upper.at[:, pl.ds(q * TILE, TILE)], recv_home.at[q])
        store(q).start()

    def near_all(q):
        for bp in range(pairs):
            for d in near_order:
                near_start(q, bp, d)

    kick_chunk(jnp.int32(0))
    pl.semaphore_wait(barrier, devices - 1)
    near_all(jnp.int32(0))

    def rad_copy(n):
        to = flip(at_b, n, bits_b)
        return pltpu.make_async_remote_copy(
            src_ref=radial_ref.at[:, pl.ds(pl.multiple_of(to * TILE, TILE), TILE)], dst_ref=far.at[at_b],
            send_sem=rad_send, recv_sem=rad_recv, device_id=(at_a, to), device_id_type=MESH,
        )

    pltpu.make_async_copy(
        radial_ref.at[:, pl.ds(pl.multiple_of(at_b * TILE, TILE), TILE)], far.at[at_b], rad_recv
    ).start()

    def rad_start(n, carry):
        rad_copy(n).start()
        return carry

    lax.fori_loop(1, rb, rad_start, 0)

    for source, target in ((first_ref, first_mat), (second_ref, second_mat)):
        target[:depth, :depth] = source[0]
        target[depth:, depth:] = source[0]
        target[:depth, depth:] = -source[1]
        target[depth:, :depth] = source[1]

    def opening(t, carry):
        @pl.when(t < chunks)
        def _():
            kick_chunk(t)
            near_all(t)

        def one(c, carry):
            first_chunk(c)
            far_start(c, 0, False)
            far_start(c, 1, False)
            return carry

        lax.fori_loop((t - 1) * pairs, t * pairs, one, 0)
        return carry

    lax.fori_loop(1, chunks + 1, opening, 0)
    def crossing(c, h):
        far_start(c, h, True)
        return h

    lax.fori_loop(0, chunks * pairs, crossing, 0)
    lax.fori_loop(0, FAR_LEAD, crossing, 1)

    arrived(lower.at[:, 0:lower.shape[1] * (ra - 1) // ra], send_sem.at[0])
    arrived(far, rad_recv)

    width = LANES * 1
    sheets = channels // width
    block = a_tiles * TILE

    def middle(h, carry):
        arrived(upper.at[:, pl.ds(h * halfway, halfway)], recv_far.at[h])

        @pl.when(h == 0)
        def _():
            lax.fori_loop(FAR_LEAD, chunks * pairs, crossing, 1)

        pieces = far[:, :, pl.ds(pl.multiple_of(h * HALF, HALF), HALF)].reshape(rb * KTERMS, HALF, b_rows)
        lines[...] = jnp.swapaxes(pieces, 0, 1)

        def spread(m, carry):
            for p in range(2):
                wide = upper[p, h * halfway + m].astype(jnp.float32).reshape(block, channels)
                for s in range(sheets):
                    turn[p, s, pl.ds(pl.multiple_of(m * block, block), block)] = wide[:, s * width:(s + 1) * width]
            return carry

        lax.fori_loop(0, halfway, spread, 0)

        def line(a, carry):
            size = second_ref.shape[1]
            at = pl.ds(a, size, stride=HALF)
            both = jnp.concatenate([
                jnp.concatenate([turn[p, s, at] for s in range(sheets)], axis=1).astype(jnp.bfloat16) for p in range(2)
            ], axis=0)
            made = jnp.dot(second_mat[...], both, preferred_element_type=jnp.float32).astype(jnp.bfloat16)
            laid = jnp.transpose(lines[a])

            def factor_of(k):
                return jnp.concatenate([
                    jnp.broadcast_to(laid[:, n * KTERMS + k:n * KTERMS + k + 1], (b_rows, channels)) for n in range(rb)
                ], axis=0)

            kicked = kick([made[:size], made[size:]], factor_of, size)
            both = jnp.concatenate([x.astype(jnp.bfloat16) for x in kicked], axis=0)
            made = jnp.dot(second_mat[...], both, preferred_element_type=jnp.float32)
            for p in range(2):
                for s in range(sheets):
                    turn[p, s, at] = made[p * size:(p + 1) * size, s * width:(s + 1) * width]
            return carry

        lax.fori_loop(0, HALF, line, 0)

        def gather(m, carry):
            for p in range(2):
                wide = jnp.concatenate([
                    turn[p, s, pl.ds(pl.multiple_of(m * block, block), block)] for s in range(sheets)
                ], axis=1)
                lower[p, h * halfway + m] = wide.astype(jnp.bfloat16).reshape(a_tiles, TILE, channels)
            return carry

        lax.fori_loop(0, halfway, gather, 0)

        every(lambda c: back_start(c, h, True))
        return carry

    lax.fori_loop(0, 2, middle, 0)

    def rest(c, carry):
        back_start(c, 0, False)
        back_start(c, 1, False)
        return carry

    lax.fori_loop(0, BACK_LEAD, rest, 0)
    arrived(right.at[:, :, :, :, 0:sixteens * (devices - 1) // devices], send_sem.at[1])

    def closing(t, carry):
        @pl.when(t < chunks)
        def _():
            def one(c, carry):
                last_chunk(c)
                for d in near_order:
                    home_start(t, lax.rem(c, pairs), d)

                @pl.when(c + BACK_LEAD < chunks * pairs)
                def _():
                    rest(c + BACK_LEAD, 0)

                return carry

            lax.fori_loop(t * pairs, (t + 1) * pairs, one, 0)

        @pl.when(t >= 1)
        def _():
            finish_chunk(t - 1)

        return carry

    lax.fori_loop(0, chunks + 1, closing, 0)

    pltpu.make_async_copy(upper, out_ref, store_sem).wait()
    arrived(lower.at[:, 0:lower.shape[1] * (devices - 1) // devices], send_sem.at[2])
    arrived(right.at[:, :, :, :, 0:sixteens * (ra - 1) // ra], send_sem.at[3])
    arrived(far.at[0:rb - 1], rad_send)


def unfold_kernel(in_ref, out_ref):
    def group(g, carry):
        for p in range(2):
            turned = jnp.swapaxes(in_ref[p, :, g].astype(jnp.float32), 0, 1)
            out_ref[p, pl.ds(g * TILE, TILE)] = turned.astype(jnp.bfloat16)
        return carry

    lax.fori_loop(0, in_ref.shape[2], group, 0)


def unfold(folded, shape):
    tiles = shape[1] // TILE
    part = tiles // 2
    return pl.pallas_call(
        unfold_kernel,
        grid=(shape[2] // TILE, tiles // part),
        in_specs=[pl.BlockSpec((2, TILE, part, TILE, shape[3]), lambda q, g: (0, q, g, 0, 0))],
        out_specs=pl.BlockSpec((2, part * TILE, TILE, shape[3]), lambda q, g: (0, g, q, 0)),
        out_shape=jax.ShapeDtypeStruct(shape, jnp.bfloat16),
    )(folded)


def on_device(amplitude, coupling, pattern, radial, first_prop, second_prop):
    a_rows, b_rows, channels = amplitude.shape[1:]
    n_a, n_b = first_prop.shape[1], second_prop.shape[1]
    ra, rb = lax.axis_size("ra"), lax.axis_size("rb")
    devices = ra * rb
    chunks = b_rows // TILE
    fits = (
        channels == 2 * LANES and ra & (ra - 1) == 0 and rb == HALF and ra in (2, 4) and n_a == n_b
        and n_a == TILE * devices and n_b == TILE * devices and a_rows % TILE == 0 and b_rows % TILE == 0
        and chunks % 2 == 0 and chunks == ra and a_rows == TILE * HALF and b_rows <= LANES
    )
    if not fits:
        return plain(amplitude, coupling, pattern, radial, first_prop, second_prop)

    pairs = TILE // ra // 2
    groups = n_a // HALF
    flat = (2, chunks * TILE, a_rows // TILE, TILE, channels)
    tall = (2, chunks, pairs, 2, groups // 2, TILE, channels)
    whole = pl.BlockSpec(memory_space=pltpu.VMEM)
    kept = pl.BlockSpec(memory_space=pl.ANY)
    dma = pltpu.SemaphoreType.DMA
    folded = pl.pallas_call(
        functools.partial(fused_kernel, ra, rb),
        in_specs=[kept, whole, pl.BlockSpec(memory_space=pltpu.SMEM), whole, whole, whole],
        out_specs=kept,
        out_shape=jax.ShapeDtypeStruct(flat, jnp.bfloat16),
        scratch_shapes=[
            pltpu.VMEM(flat, jnp.bfloat16),
            pltpu.VMEM(flat, jnp.bfloat16),
            pltpu.VMEM(tall, jnp.bfloat16),
            pltpu.VMEM(tall, jnp.bfloat16),
            pltpu.VMEM((2, channels // LANES, n_b * HALF, LANES), jnp.float32),
            pltpu.VMEM((2, 2, a_rows, TILE, channels), jnp.bfloat16),
            pltpu.VMEM((2 * n_a, 2 * n_a), jnp.bfloat16),
            pltpu.VMEM((2 * n_b, 2 * n_b), jnp.bfloat16),
            pltpu.VMEM((KTERMS, channels, channels), jnp.bfloat16),
            pltpu.VMEM((KTERMS, a_rows, b_rows), jnp.float32),
            pltpu.VMEM((a_rows // HALF, b_rows, KTERMS * HALF), jnp.float32),
            pltpu.VMEM((rb, KTERMS, TILE, b_rows), jnp.float32),
            pltpu.VMEM((HALF, rb * KTERMS, b_rows), jnp.float32),
            dma((2,)), dma(()), dma((4,)), dma((chunks * pairs,)), dma((2,)), dma((chunks * pairs,)), dma((chunks,)),
            dma(()), dma(()),
        ],
        compiler_params=pltpu.CompilerParams(
            collective_id=0, has_side_effects=True, vmem_limit_bytes=63 * 2**20
        ),
    )(amplitude, coupling, pattern.transpose(1, 2, 0), radial.transpose(0, 2, 1), first_prop, second_prop)
    return unfold(folded, amplitude.shape)


def solution(mesh):
    return jax.shard_map(
        on_device,
        mesh=mesh,
        in_specs=(P(None, "ra", "rb", None), P(), P(), P(None, "ra", "rb"), P(), P()),
        out_specs=P(None, "ra", "rb", None),
        check_vma=False,
    )
```

```python
import functools

import jax
import jax.numpy as jnp
from jax import lax
from jax.experimental import pallas as pl
from jax.experimental.pallas import tpu as pltpu
from jax.sharding import PartitionSpec as P

KTERMS = 6
STEPS = 2
LANES = 128
TILE = 16
HALF = 8
MESH = pl.DeviceIdType.MESH


def complex_rows(matrix, piece):
    form = "ac,cqw->aqw"
    real_part = jnp.einsum(
        form, matrix[0], piece[0], preferred_element_type=jnp.float32
    ) - jnp.einsum(form, matrix[1], piece[1], preferred_element_type=jnp.float32)
    imag_part = jnp.einsum(
        form, matrix[0], piece[1], preferred_element_type=jnp.float32
    ) + jnp.einsum(form, matrix[1], piece[0], preferred_element_type=jnp.float32)
    return jnp.stack([real_part, imag_part]).astype(jnp.bfloat16)


def masked_weights(coupling, pattern):
    channels = coupling.shape[1]
    count = pattern.shape[1]
    block_size = channels // count
    spread = jnp.broadcast_to(
        pattern[:, :, None, :, None], (KTERMS, count, block_size, count, block_size)
    )
    return coupling * spread.reshape(KTERMS, channels, channels).astype(jnp.bfloat16)


def plain(amplitude, coupling, pattern, radial, first_prop, second_prop):
    first_rows, second_rows, channels = (amplitude.shape[1], amplitude.shape[2], amplitude.shape[3])
    cells = first_rows * second_rows
    groups_a = lax.axis_size("ra")
    groups_b = lax.axis_size("rb")
    width_a = channels // groups_a
    width_b = channels // groups_b
    weights = masked_weights(coupling, pattern)
    radial_cells = radial.reshape(KTERMS, cells).T
    for sweep in range(STEPS):
        flat = amplitude.reshape(2 * cells, channels)
        applied = jnp.einsum("mj,kij->mki", flat, weights, preferred_element_type=jnp.float32)
        applied = applied.reshape(2, cells, KTERMS, channels)
        coupled = jnp.sum(applied * radial_cells[None, :, :, None], axis=2)
        wide = amplitude.reshape(2, cells, channels).astype(jnp.float32)
        kicked = jnp.stack([wide[0] + coupled[1], wide[1] - coupled[0]]).astype(jnp.bfloat16)
        grouped = kicked.reshape(2, first_rows, second_rows, groups_a, width_a)
        grouped = grouped.transpose(0, 1, 3, 2, 4).reshape(
            2, first_rows, groups_a, second_rows * width_a
        )
        half = complex_rows(
            first_prop, lax.all_to_all(grouped, "ra", split_axis=2, concat_axis=1, tiled=True)
        )
        restored = lax.all_to_all(half, "ra", split_axis=1, concat_axis=2, tiled=True)
        restored = restored.reshape(2, first_rows, groups_a, second_rows, width_a)
        restored = restored.transpose(0, 1, 3, 2, 4).reshape(
            2, first_rows, second_rows, groups_b, width_b
        )
        regrouped = restored.transpose(0, 2, 3, 1, 4).reshape(
            2, second_rows, groups_b, first_rows * width_b
        )
        moved = complex_rows(
            second_prop, lax.all_to_all(regrouped, "rb", split_axis=2, concat_axis=1, tiled=True)
        )
        settled = lax.all_to_all(moved, "rb", split_axis=1, concat_axis=2, tiled=True)
        settled = settled.reshape(2, second_rows, groups_b, first_rows, width_b)
        amplitude = settled.transpose(0, 3, 1, 2, 4).reshape(2, first_rows, second_rows, channels)
    return amplitude


BACK_LEAD = 2
FAR_LEAD = 2


def flip(value, mask, bits):
    out = 0
    for n in range(bits):
        weight = 1 << n
        out = out + lax.rem(lax.div(value, weight) + lax.div(mask, weight), 2) * weight
    return out


def fused_kernel(ra, rb, amp_ref, coupling_ref, pattern_ref, turned_ref, first_ref, second_ref, upper,
                 lower, left, right, turn, stage, first_mat, second_mat, weights_ref, radial_ref, near, far, lines,
                 load_sem, send_sem, recv_near, recv_far, recv_back, recv_home, rad_send, rad_recv):
    at_a, at_b = lax.axis_index("ra"), lax.axis_index("rb")
    bits_a, bits_b = ra.bit_length() - 1, rb.bit_length() - 1
    chunks = left.shape[1]
    pairs = left.shape[2]
    sixteens = left.shape[4]
    groups = 2 * sixteens
    per = pairs * 2
    depth = first_ref.shape[1]
    halfway = lower.shape[1] // 2
    channels = lower.shape[4]
    a_tiles = lower.shape[2]
    devices = ra * rb
    route = [("b", bits_b - 1)] + [("b", n) for n in range(bits_b - 1)]
    route = route + [("a", n) for n in range(bits_a)]

    def partner(d):
        mask_a, mask_b = 0, 0
        for n, (axis, bit) in enumerate(route):
            one = lax.rem(lax.div(d, 1 << n), 2) * (1 << bit)
            if axis == "a":
                mask_a = mask_a + one
            else:
                mask_b = mask_b + one
        return flip(at_a, mask_a, bits_a), flip(at_b, mask_b, bits_b)

    barrier = pltpu.get_barrier_semaphore()

    def greet(d, carry):
        to_a, to_b = partner(d)
        pl.semaphore_signal(barrier, inc=1, device_id=(to_a, to_b), device_id_type=MESH)
        return carry

    lax.fori_loop(1, devices, greet, 0)

    def load(q):
        slot = lax.rem(q, 2)
        return pltpu.make_async_copy(amp_ref.at[:, :, pl.ds(q * TILE, TILE)], stage.at[slot], load_sem.at[slot])

    load(jnp.int32(0)).start()
    load(jnp.int32(1)).start()

    b_rows = amp_ref.shape[2]
    blocks = pattern_ref.shape[0]
    size_block = channels // blocks
    lane = lax.broadcasted_iota(jnp.int32, (size_block, channels), 1)
    for k in range(KTERMS):
        masked = []
        for i in range(blocks):
            keep = jnp.zeros((size_block, channels), jnp.float32)
            for j in range(blocks):
                inside = (lane >= j * size_block) & (lane < (j + 1) * size_block)
                keep = jnp.where(inside, pattern_ref[i, j, k].astype(jnp.float32), keep)
            masked.append(coupling_ref[k, i * size_block:(i + 1) * size_block].astype(jnp.float32) * keep)
        weights_ref[k] = jnp.transpose(jnp.concatenate(masked, axis=0)).astype(jnp.bfloat16)

    for k in range(KTERMS):
        radial_ref[k] = jnp.transpose(turned_ref[k])

    def lay(g, carry):
        at = pl.ds(pl.multiple_of(g * HALF, HALF), HALF)
        near[g] = jnp.transpose(radial_ref[:, at].reshape(KTERMS * HALF, b_rows))
        return carry

    lax.fori_loop(0, radial_ref.shape[1] // HALF, lay, 0)

    def kick(planes, factor_of, count):
        both = jnp.concatenate(planes, axis=0)
        total = [None, None]
        for k in range(KTERMS):
            applied = jnp.dot(both, weights_ref[k], preferred_element_type=jnp.float32)
            factor = factor_of(k)
            for p in range(2):
                term = applied[p * count:(p + 1) * count] * factor
                total[p] = term if k == 0 else total[p] + term
        return planes[0].astype(jnp.float32) + total[1], planes[1].astype(jnp.float32) - total[0]

    def kick_chunk(q):
        slot = lax.rem(q, 2)
        load(q).wait()

        def group(g, carry):
            count = TILE * TILE
            planes = [stage[slot, p, pl.ds(g * TILE, TILE)].reshape(count, channels) for p in range(2)]
            laid = [near[g * 2 + n, pl.ds(pl.multiple_of(q * TILE, TILE), TILE)] for n in range(2)]

            def factor_of(k):
                return jnp.concatenate([
                    jnp.broadcast_to(laid[n // HALF][:, k * HALF + n % HALF:k * HALF + n % HALF + 1], (TILE, channels))
                    for n in range(TILE)
                ], axis=0)

            result = kick(planes, factor_of, count)
            for p in range(2):
                turned = jnp.swapaxes(result[p].reshape(TILE, TILE, channels), 0, 1).astype(jnp.bfloat16)
                lower[p, pl.ds(q * TILE, TILE), g] = turned
            return carry

        lax.fori_loop(0, a_tiles, group, 0)

        @pl.when(q + 2 < chunks)
        def _():
            load(q + 2).start()

    def near_start(q, bp, d):
        to = flip(at_a, d, bits_a)
        source = lower.at[:, pl.ds(q * TILE + to * per + bp * 2, 2)]
        target = left.at[:, q, bp, :, pl.ds(at_a * a_tiles, a_tiles)]
        sem = recv_near.at[q * pairs + bp]
        if d == 0:
            pltpu.make_async_copy(source, target, sem).start()
        else:
            pltpu.make_async_remote_copy(
                src_ref=source, dst_ref=target, send_sem=send_sem.at[0], recv_sem=sem,
                device_id=(to, at_b), device_id_type=MESH,
            ).start()

    def home_start(q, bp, d):
        to = flip(at_a, d, bits_a)
        source = right.at[:, q, bp, :, pl.ds(to * a_tiles, a_tiles)]
        target = upper.at[:, pl.ds(q * TILE + at_a * per + bp * 2, 2)]
        if d == 0:
            pltpu.make_async_copy(source, target, recv_home.at[q]).start()
        else:
            pltpu.make_async_remote_copy(
                src_ref=source, dst_ref=target, send_sem=send_sem.at[3], recv_sem=recv_home.at[q],
                device_id=(to, at_b), device_id_type=MESH,
            ).start()

    near_order = list(range(ra // 2, ra)) + list(range(1, ra // 2)) + [0]
    side = devices // 2

    def place(i, j, h):
        index = (i * rb + j) * 2 + h
        return lax.div(index, sixteens), lax.rem(index, sixteens)

    def far_start(c, h, crossing):
        q, bp = lax.div(c, pairs), lax.rem(c, pairs)
        row = h * halfway + at_b * chunks + q
        target = upper.at[:, row, at_a * pairs + bp]

        def one(d, carry):
            to_a, to_b = partner(d)
            high, low = place(to_a, to_b, h)
            pltpu.make_async_remote_copy(
                src_ref=right.at[:, q, bp, high, low], dst_ref=target,
                send_sem=send_sem.at[1], recv_sem=recv_far.at[h], device_id=(to_a, to_b), device_id_type=MESH,
            ).start()
            return carry

        if crossing:
            lax.fori_loop(side, devices, one, 0)
        else:
            lax.fori_loop(1, side, one, 0)
            high, low = place(at_a, at_b, h)
            pltpu.make_async_copy(right.at[:, q, bp, high, low], target, recv_far.at[h]).start()

    def back_start(c, h, crossing):
        q, bp = lax.div(c, pairs), lax.rem(c, pairs)
        high, low = place(at_a, at_b, h)
        target = left.at[:, q, bp, high, low]

        def one(d, carry):
            to_a, to_b = partner(d)
            pltpu.make_async_remote_copy(
                src_ref=lower.at[:, h * halfway + to_b * chunks + q, to_a * pairs + bp], dst_ref=target,
                send_sem=send_sem.at[2], recv_sem=recv_back.at[c], device_id=(to_a, to_b), device_id_type=MESH,
            ).start()
            return carry

        if crossing:
            lax.fori_loop(side, devices, one, 0)
        else:
            lax.fori_loop(1, side, one, 0)
            pltpu.make_async_copy(
                lower.at[:, h * halfway + at_b * chunks + q, at_a * pairs + bp], target, recv_back.at[c]
            ).start()

    def every(action):
        def one(c, carry):
            action(c)
            return carry

        lax.fori_loop(0, chunks * pairs, one, 0)

    def arrived(ref, sem):
        pltpu.make_async_copy(ref, ref, sem).wait()

    def first_chunk(c):
        q, bp = lax.div(c, pairs), lax.rem(c, pairs)
        arrived(left.at[:, q, bp], recv_near.at[c])
        made = []
        for par in range(2):
            both = jnp.concatenate([left[p, q, bp, par].reshape(depth, channels) for p in range(2)], axis=0)
            made.append(jnp.dot(first_mat[...], both, preferred_element_type=jnp.float32))
        for p in range(2):
            parts = [m[p * depth:(p + 1) * depth].reshape(groups, HALF, channels) for m in made]
            mixed = jnp.concatenate(parts, axis=1).astype(jnp.bfloat16)
            right[p, q, bp] = mixed.reshape(2, sixteens, TILE, channels)

    def last_chunk(c):
        q, bp = lax.div(c, pairs), lax.rem(c, pairs)
        arrived(left.at[:, q, bp], recv_back.at[c])
        wide = [left[p, q, bp].reshape(groups, TILE, channels).astype(jnp.float32) for p in range(2)]
        for par in range(2):
            both = jnp.concatenate([
                w[:, par * HALF:(par + 1) * HALF].reshape(depth, channels).astype(jnp.bfloat16) for w in wide
            ], axis=0)
            made = jnp.dot(first_mat[...], both, preferred_element_type=jnp.float32)
            for p in range(2):
                part = made[p * depth:(p + 1) * depth].reshape(sixteens, TILE, channels)
                right[p, q, bp, par] = part.astype(jnp.bfloat16)

    def finish_chunk(q):
        arrived(upper.at[:, pl.ds(q * TILE, TILE)], recv_home.at[q])

    def near_all(q):
        for bp in range(pairs):
            for d in near_order:
                near_start(q, bp, d)

    kick_chunk(jnp.int32(0))
    pl.semaphore_wait(barrier, devices - 1)
    near_all(jnp.int32(0))

    def rad_copy(n):
        to = flip(at_b, n, bits_b)
        return pltpu.make_async_remote_copy(
            src_ref=radial_ref.at[:, pl.ds(pl.multiple_of(to * TILE, TILE), TILE)], dst_ref=far.at[at_b],
            send_sem=rad_send, recv_sem=rad_recv, device_id=(at_a, to), device_id_type=MESH,
        )

    pltpu.make_async_copy(
        radial_ref.at[:, pl.ds(pl.multiple_of(at_b * TILE, TILE), TILE)], far.at[at_b], rad_recv
    ).start()

    def rad_start(n, carry):
        rad_copy(n).start()
        return carry

    lax.fori_loop(1, rb, rad_start, 0)

    for source, target in ((first_ref, first_mat), (second_ref, second_mat)):
        target[:depth, :depth] = source[0]
        target[depth:, depth:] = source[0]
        target[:depth, depth:] = -source[1]
        target[depth:, :depth] = source[1]

    def opening(t, carry):
        @pl.when(t < chunks)
        def _():
            kick_chunk(t)
            near_all(t)

        def one(c, carry):
            first_chunk(c)
            far_start(c, 0, False)
            far_start(c, 1, False)
            return carry

        lax.fori_loop((t - 1) * pairs, t * pairs, one, 0)
        return carry

    lax.fori_loop(1, chunks + 1, opening, 0)
    def crossing(c, h):
        far_start(c, h, True)
        return h

    lax.fori_loop(0, chunks * pairs, crossing, 0)
    lax.fori_loop(0, FAR_LEAD, crossing, 1)

    arrived(lower.at[:, 0:lower.shape[1] * (ra - 1) // ra], send_sem.at[0])
    arrived(far, rad_recv)

    width = LANES * 1
    sheets = channels // width
    block = a_tiles * TILE

    def middle(h, carry):
        arrived(upper.at[:, pl.ds(h * halfway, halfway)], recv_far.at[h])

        @pl.when(h == 0)
        def _():
            lax.fori_loop(FAR_LEAD, chunks * pairs, crossing, 1)

        pieces = far[:, :, pl.ds(pl.multiple_of(h * HALF, HALF), HALF)].reshape(rb * KTERMS, HALF, b_rows)
        lines[...] = jnp.swapaxes(pieces, 0, 1)

        def spread(m, carry):
            for p in range(2):
                wide = upper[p, h * halfway + m].astype(jnp.float32).reshape(block, channels)
                for s in range(sheets):
                    turn[p, s, pl.ds(pl.multiple_of(m * block, block), block)] = wide[:, s * width:(s + 1) * width]
            return carry

        lax.fori_loop(0, halfway, spread, 0)

        def line(a, carry):
            size = second_ref.shape[1]
            at = pl.ds(a, size, stride=HALF)
            both = jnp.concatenate([
                jnp.concatenate([turn[p, s, at] for s in range(sheets)], axis=1).astype(jnp.bfloat16) for p in range(2)
            ], axis=0)
            made = jnp.dot(second_mat[...], both, preferred_element_type=jnp.float32).astype(jnp.bfloat16)
            laid = jnp.transpose(lines[a])

            def factor_of(k):
                return jnp.concatenate([
                    jnp.broadcast_to(laid[:, n * KTERMS + k:n * KTERMS + k + 1], (b_rows, channels)) for n in range(rb)
                ], axis=0)

            kicked = kick([made[:size], made[size:]], factor_of, size)
            both = jnp.concatenate([x.astype(jnp.bfloat16) for x in kicked], axis=0)
            made = jnp.dot(second_mat[...], both, preferred_element_type=jnp.float32)
            for p in range(2):
                for s in range(sheets):
                    turn[p, s, at] = made[p * size:(p + 1) * size, s * width:(s + 1) * width]
            return carry

        lax.fori_loop(0, HALF, line, 0)

        def gather(m, carry):
            for p in range(2):
                wide = jnp.concatenate([
                    turn[p, s, pl.ds(pl.multiple_of(m * block, block), block)] for s in range(sheets)
                ], axis=1)
                lower[p, h * halfway + m] = wide.astype(jnp.bfloat16).reshape(a_tiles, TILE, channels)
            return carry

        lax.fori_loop(0, halfway, gather, 0)

        every(lambda c: back_start(c, h, True))
        return carry

    lax.fori_loop(0, 2, middle, 0)

    def rest(c, carry):
        back_start(c, 0, False)
        back_start(c, 1, False)
        return carry

    lax.fori_loop(0, BACK_LEAD, rest, 0)
    arrived(right.at[:, :, :, :, 0:sixteens * (devices - 1) // devices], send_sem.at[1])

    def closing(t, carry):
        @pl.when(t < chunks)
        def _():
            def one(c, carry):
                last_chunk(c)
                for d in near_order:
                    home_start(t, lax.rem(c, pairs), d)

                @pl.when(c + BACK_LEAD < chunks * pairs)
                def _():
                    rest(c + BACK_LEAD, 0)

                return carry

            lax.fori_loop(t * pairs, (t + 1) * pairs, one, 0)

        @pl.when(t >= 1)
        def _():
            finish_chunk(t - 1)

        return carry

    lax.fori_loop(0, chunks + 1, closing, 0)

    arrived(lower.at[:, 0:lower.shape[1] * (devices - 1) // devices], send_sem.at[2])
    arrived(right.at[:, :, :, :, 0:sixteens * (ra - 1) // ra], send_sem.at[3])
    arrived(far.at[0:rb - 1], rad_send)


def unfold_kernel(in_ref, out_ref, stage, sem):
    chunks = stage.shape[0]
    tiles = stage.shape[2] // TILE
    part = tiles // 2

    def piece(n, carry):
        q, first = lax.div(n, 2), lax.rem(n, 2) * part
        for g in range(part):
            for p in range(2):
                rows = in_ref[p, pl.ds(q * TILE, TILE), first + g]
                turned = jnp.swapaxes(rows.astype(jnp.float32), 0, 1)
                stage[q, p, pl.ds((first + g) * TILE, TILE)] = turned.astype(jnp.bfloat16)
        span = pl.ds(first * TILE, part * TILE)
        pltpu.make_async_copy(
            stage.at[q, :, span], out_ref.at[:, span, pl.ds(pl.multiple_of(q * TILE, TILE), TILE)], sem
        ).start()
        return carry

    lax.fori_loop(0, 2 * chunks, piece, 0)
    pltpu.make_async_copy(stage, stage, sem).wait()


def unfold(folded, shape):
    return pl.pallas_call(
        unfold_kernel,
        in_specs=[pl.BlockSpec(memory_space=pltpu.VMEM)],
        out_specs=pl.BlockSpec(memory_space=pl.ANY),
        out_shape=jax.ShapeDtypeStruct(shape, jnp.bfloat16),
        scratch_shapes=[
            pltpu.VMEM((shape[2] // TILE, 2, shape[1], TILE, shape[3]), jnp.bfloat16),
            pltpu.SemaphoreType.DMA(()),
        ],
        compiler_params=pltpu.CompilerParams(vmem_limit_bytes=24 * 2**20),
    )(folded)


def on_device(amplitude, coupling, pattern, radial, first_prop, second_prop):
    a_rows, b_rows, channels = amplitude.shape[1:]
    n_a, n_b = first_prop.shape[1], second_prop.shape[1]
    ra, rb = lax.axis_size("ra"), lax.axis_size("rb")
    devices = ra * rb
    chunks = b_rows // TILE
    fits = (
        channels == 2 * LANES and ra & (ra - 1) == 0 and rb == HALF and ra in (2, 4) and n_a == n_b
        and n_a == TILE * devices and n_b == TILE * devices and a_rows % TILE == 0 and b_rows % TILE == 0
        and chunks % 2 == 0 and chunks == ra and a_rows == TILE * HALF and b_rows <= LANES
    )
    if not fits:
        return plain(amplitude, coupling, pattern, radial, first_prop, second_prop)

    pairs = TILE // ra // 2
    groups = n_a // HALF
    flat = (2, chunks * TILE, a_rows // TILE, TILE, channels)
    tall = (2, chunks, pairs, 2, groups // 2, TILE, channels)
    whole = pl.BlockSpec(memory_space=pltpu.VMEM)
    kept = pl.BlockSpec(memory_space=pl.ANY)
    dma = pltpu.SemaphoreType.DMA
    folded = pl.pallas_call(
        functools.partial(fused_kernel, ra, rb),
        in_specs=[kept, whole, pl.BlockSpec(memory_space=pltpu.SMEM), whole, whole, whole],
        out_specs=whole,
        out_shape=pltpu.VMEM(flat, jnp.bfloat16),
        scratch_shapes=[
            pltpu.VMEM(flat, jnp.bfloat16),
            pltpu.VMEM(tall, jnp.bfloat16),
            pltpu.VMEM(tall, jnp.bfloat16),
            pltpu.VMEM((2, channels // LANES, n_b * HALF, LANES), jnp.float32),
            pltpu.VMEM((2, 2, a_rows, TILE, channels), jnp.bfloat16),
            pltpu.VMEM((2 * n_a, 2 * n_a), jnp.bfloat16),
            pltpu.VMEM((2 * n_b, 2 * n_b), jnp.bfloat16),
            pltpu.VMEM((KTERMS, channels, channels), jnp.bfloat16),
            pltpu.VMEM((KTERMS, a_rows, b_rows), jnp.float32),
            pltpu.VMEM((a_rows // HALF, b_rows, KTERMS * HALF), jnp.float32),
            pltpu.VMEM((rb, KTERMS, TILE, b_rows), jnp.float32),
            pltpu.VMEM((HALF, rb * KTERMS, b_rows), jnp.float32),
            dma((2,)), dma((4,)), dma((chunks * pairs,)), dma((2,)), dma((chunks * pairs,)), dma((chunks,)),
            dma(()), dma(()),
        ],
        compiler_params=pltpu.CompilerParams(
            collective_id=0, has_side_effects=True, vmem_limit_bytes=55 * 2**20
        ),
    )(amplitude, coupling, pattern.transpose(1, 2, 0), radial.transpose(0, 2, 1), first_prop, second_prop)
    return unfold(folded, amplitude.shape)


def solution(mesh):
    return jax.shard_map(
        on_device,
        mesh=mesh,
        in_specs=(P(None, "ra", "rb", None), P(), P(), P(None, "ra", "rb"), P(), P()),
        out_specs=P(None, "ra", "rb", None),
        check_vma=False,
    )
```

```python
import functools

import jax
import jax.numpy as jnp
from jax import lax
from jax.experimental import pallas as pl
from jax.experimental.pallas import tpu as pltpu
from jax.sharding import PartitionSpec as P

KTERMS = 6
STEPS = 2
LANES = 128
TILE = 16
HALF = 8
MESH = pl.DeviceIdType.MESH


def complex_rows(matrix, piece):
    form = "ac,cqw->aqw"
    real_part = jnp.einsum(
        form, matrix[0], piece[0], preferred_element_type=jnp.float32
    ) - jnp.einsum(form, matrix[1], piece[1], preferred_element_type=jnp.float32)
    imag_part = jnp.einsum(
        form, matrix[0], piece[1], preferred_element_type=jnp.float32
    ) + jnp.einsum(form, matrix[1], piece[0], preferred_element_type=jnp.float32)
    return jnp.stack([real_part, imag_part]).astype(jnp.bfloat16)


def masked_weights(coupling, pattern):
    channels = coupling.shape[1]
    count = pattern.shape[1]
    block_size = channels // count
    spread = jnp.broadcast_to(
        pattern[:, :, None, :, None], (KTERMS, count, block_size, count, block_size)
    )
    return coupling * spread.reshape(KTERMS, channels, channels).astype(jnp.bfloat16)


def plain(amplitude, coupling, pattern, radial, first_prop, second_prop):
    first_rows, second_rows, channels = (amplitude.shape[1], amplitude.shape[2], amplitude.shape[3])
    cells = first_rows * second_rows
    groups_a = lax.axis_size("ra")
    groups_b = lax.axis_size("rb")
    width_a = channels // groups_a
    width_b = channels // groups_b
    weights = masked_weights(coupling, pattern)
    radial_cells = radial.reshape(KTERMS, cells).T
    for sweep in range(STEPS):
        flat = amplitude.reshape(2 * cells, channels)
        applied = jnp.einsum("mj,kij->mki", flat, weights, preferred_element_type=jnp.float32)
        applied = applied.reshape(2, cells, KTERMS, channels)
        coupled = jnp.sum(applied * radial_cells[None, :, :, None], axis=2)
        wide = amplitude.reshape(2, cells, channels).astype(jnp.float32)
        kicked = jnp.stack([wide[0] + coupled[1], wide[1] - coupled[0]]).astype(jnp.bfloat16)
        grouped = kicked.reshape(2, first_rows, second_rows, groups_a, width_a)
        grouped = grouped.transpose(0, 1, 3, 2, 4).reshape(
            2, first_rows, groups_a, second_rows * width_a
        )
        half = complex_rows(
            first_prop, lax.all_to_all(grouped, "ra", split_axis=2, concat_axis=1, tiled=True)
        )
        restored = lax.all_to_all(half, "ra", split_axis=1, concat_axis=2, tiled=True)
        restored = restored.reshape(2, first_rows, groups_a, second_rows, width_a)
        restored = restored.transpose(0, 1, 3, 2, 4).reshape(
            2, first_rows, second_rows, groups_b, width_b
        )
        regrouped = restored.transpose(0, 2, 3, 1, 4).reshape(
            2, second_rows, groups_b, first_rows * width_b
        )
        moved = complex_rows(
            second_prop, lax.all_to_all(regrouped, "rb", split_axis=2, concat_axis=1, tiled=True)
        )
        settled = lax.all_to_all(moved, "rb", split_axis=1, concat_axis=2, tiled=True)
        settled = settled.reshape(2, second_rows, groups_b, first_rows, width_b)
        amplitude = settled.transpose(0, 3, 1, 2, 4).reshape(2, first_rows, second_rows, channels)
    return amplitude


FAR_LEAD = 2


def flip(value, mask, bits):
    out = 0
    for n in range(bits):
        weight = 1 << n
        out = out + lax.rem(lax.div(value, weight) + lax.div(mask, weight), 2) * weight
    return out


def fused_kernel(ra, rb, amp_ref, coupling_ref, pattern_ref, turned_ref, first_ref, second_ref, upper,
                 lower, left, right, turn, stage, first_mat, second_mat, weights_ref, radial_ref, near, far, lines,
                 load_sem, send_sem, recv_near, recv_far, recv_back, recv_home, rad_send, rad_recv):
    at_a, at_b = lax.axis_index("ra"), lax.axis_index("rb")
    bits_a, bits_b = ra.bit_length() - 1, rb.bit_length() - 1
    chunks = left.shape[1]
    pairs = left.shape[2]
    sixteens = left.shape[4]
    groups = 2 * sixteens
    per = pairs * 2
    depth = first_ref.shape[1]
    halfway = lower.shape[1] // 2
    channels = lower.shape[4]
    a_tiles = lower.shape[2]
    devices = ra * rb
    route = [("b", bits_b - 1)] + [("b", n) for n in range(bits_b - 1)]
    route = route + [("a", n) for n in range(bits_a)]

    def partner(d):
        mask_a, mask_b = 0, 0
        for n, (axis, bit) in enumerate(route):
            one = lax.rem(lax.div(d, 1 << n), 2) * (1 << bit)
            if axis == "a":
                mask_a = mask_a + one
            else:
                mask_b = mask_b + one
        return flip(at_a, mask_a, bits_a), flip(at_b, mask_b, bits_b)

    barrier = pltpu.get_barrier_semaphore()

    def greet(d, carry):
        to_a, to_b = partner(devices - d)
        pl.semaphore_signal(barrier, inc=1, device_id=(to_a, to_b), device_id_type=MESH)
        return carry

    lax.fori_loop(1, devices, greet, 0)

    every_lane = pl.ds(0, channels)
    sheets = channels // LANES
    sheet = [pl.ds(s * LANES, LANES) for s in range(sheets)]
    last = chunks * pairs

    def edge(c):
        return (c == 0) | (c == last - 1)

    def spare(c, s):
        return last + lax.div(c, last - 1) * sheets + s

    def load(q):
        slot = lax.rem(q, 2)
        return pltpu.make_async_copy(amp_ref.at[:, :, pl.ds(q * TILE, TILE)], stage.at[slot], load_sem.at[slot])

    load(jnp.int32(0)).start()
    load(jnp.int32(1)).start()

    b_rows = amp_ref.shape[2]
    blocks = pattern_ref.shape[0]
    size_block = channels // blocks
    lane = lax.broadcasted_iota(jnp.int32, (size_block, channels), 1)
    for k in range(KTERMS):
        masked = []
        for i in range(blocks):
            keep = jnp.zeros((size_block, channels), jnp.float32)
            for j in range(blocks):
                inside = (lane >= j * size_block) & (lane < (j + 1) * size_block)
                keep = jnp.where(inside, pattern_ref[i, j, k].astype(jnp.float32), keep)
            masked.append(coupling_ref[k, i * size_block:(i + 1) * size_block].astype(jnp.float32) * keep)
        weights_ref[k] = jnp.transpose(jnp.concatenate(masked, axis=0)).astype(jnp.bfloat16)

    for k in range(KTERMS):
        radial_ref[k] = jnp.transpose(turned_ref[k])

    def lay(g, carry):
        at = pl.ds(pl.multiple_of(g * HALF, HALF), HALF)
        near[g] = jnp.transpose(radial_ref[:, at].reshape(KTERMS * HALF, b_rows))
        return carry

    lax.fori_loop(0, radial_ref.shape[1] // HALF, lay, 0)

    def kick(planes, factor_of, count):
        both = jnp.concatenate(planes, axis=0)
        total = [None, None]
        for k in range(KTERMS):
            applied = jnp.dot(both, weights_ref[k], preferred_element_type=jnp.float32)
            factor = factor_of(k)
            for p in range(2):
                term = applied[p * count:(p + 1) * count] * factor
                total[p] = term if k == 0 else total[p] + term
        return planes[0].astype(jnp.float32) + total[1], planes[1].astype(jnp.float32) - total[0]

    def kick_chunk(q, first=0, stop=None):
        slot = lax.rem(q, 2)
        if first == 0:
            load(q).wait()

        def group(g, carry):
            count = TILE * TILE
            planes = [stage[slot, p, pl.ds(g * TILE, TILE)].reshape(count, channels) for p in range(2)]
            laid = [near[g * 2 + n, pl.ds(pl.multiple_of(q * TILE, TILE), TILE)] for n in range(2)]

            def factor_of(k):
                return jnp.concatenate([
                    jnp.broadcast_to(laid[n // HALF][:, k * HALF + n % HALF:k * HALF + n % HALF + 1], (TILE, channels))
                    for n in range(TILE)
                ], axis=0)

            result = kick(planes, factor_of, count)
            for p in range(2):
                turned = jnp.swapaxes(result[p].reshape(TILE, TILE, channels), 0, 1).astype(jnp.bfloat16)
                lower[p, pl.ds(q * TILE, TILE), g] = turned
            return carry

        lax.fori_loop(first, a_tiles if stop is None else stop, group, 0)
        if stop is None:
            @pl.when(q + 2 < chunks)
            def _():
                load(q + 2).start()

    def near_start(q, bp, d, first=0, count=None, lanes=every_lane, sem=None):
        to = flip(at_a, d, bits_a) if d < ra // 2 else opposite + d - ra // 2
        count = a_tiles if count is None else count
        source = lower.at[:, pl.ds(q * TILE + to * per + bp * 2, 2), pl.ds(first, count), :, lanes]
        target = left.at[:, q, bp, :, pl.ds(at_a * a_tiles + first, count), :, lanes]
        sem = recv_near.at[q * pairs + bp if sem is None else sem]
        if d == 0:
            pltpu.make_async_copy(source, target, sem).start()
        else:
            pltpu.make_async_remote_copy(
                src_ref=source, dst_ref=target, send_sem=send_sem.at[0], recv_sem=sem,
                device_id=(to, at_b), device_id_type=MESH,
            ).start()

    def home_start(q, bp, d, lanes=every_lane):
        to = flip(at_a, d, bits_a)
        source = right.at[:, q, bp, :, pl.ds(to * a_tiles, a_tiles), :, lanes]
        target = upper.at[:, pl.ds(q * TILE + at_a * per + bp * 2, 2), :, :, lanes]
        if d == 0:
            pltpu.make_async_copy(source, target, recv_home.at[q]).start()
        else:
            pltpu.make_async_remote_copy(
                src_ref=source, dst_ref=target, send_sem=send_sem.at[3], recv_sem=recv_home.at[q],
                device_id=(to, at_b), device_id_type=MESH,
            ).start()

    opposite = (1 - lax.div(at_a, ra // 2)) * (ra // 2)
    near_order = list(range(ra // 2, ra)) + list(range(1, ra // 2)) + [0]
    side = devices // 2

    def place(i, j, h):
        index = (i * rb + j) * 2 + h
        return lax.div(index, sixteens), lax.rem(index, sixteens)

    def far_start(c, h, crossing, lanes=every_lane):
        q, bp = lax.div(c, pairs), lax.rem(c, pairs)
        row = h * halfway + at_b * chunks + q
        target = upper.at[:, row, at_a * pairs + bp, :, lanes]

        def one(d, carry):
            to_a, to_b = partner(d)
            high, low = place(to_a, to_b, h)
            pltpu.make_async_remote_copy(
                src_ref=right.at[:, q, bp, high, low, :, lanes], dst_ref=target,
                send_sem=send_sem.at[1], recv_sem=recv_far.at[h], device_id=(to_a, to_b), device_id_type=MESH,
            ).start()
            return carry

        if crossing:
            lax.fori_loop(side, devices, one, 0)
        else:
            lax.fori_loop(1, side, one, 0)
            high, low = place(at_a, at_b, h)
            pltpu.make_async_copy(right.at[:, q, bp, high, low, :, lanes], target, recv_far.at[h]).start()

    def back_start(c, h, crossing, lanes=every_lane, sem=None):
        q, bp = lax.div(c, pairs), lax.rem(c, pairs)
        high, low = place(at_a, at_b, h)
        target = left.at[:, q, bp, high, low, :, lanes]
        sem = recv_back.at[c if sem is None else sem]

        def one(d, carry):
            to_a, to_b = partner(d)
            pltpu.make_async_remote_copy(
                src_ref=lower.at[:, h * halfway + to_b * chunks + q, to_a * pairs + bp, :, lanes], dst_ref=target,
                send_sem=send_sem.at[2], recv_sem=sem, device_id=(to_a, to_b), device_id_type=MESH,
            ).start()
            return carry

        if crossing:
            lax.fori_loop(side, devices, one, 0)
        else:
            lax.fori_loop(1, side, one, 0)
            pltpu.make_async_copy(
                lower.at[:, h * halfway + at_b * chunks + q, at_a * pairs + bp, :, lanes], target, sem
            ).start()

    def every(action):
        def one(c, carry):
            action(c)
            return carry

        lax.fori_loop(0, chunks * pairs, one, 0)

    def arrived(ref, sem):
        pltpu.make_async_copy(ref, ref, sem).wait()

    def first_chunk(c, lanes=every_lane, sem=None):
        q, bp = lax.div(c, pairs), lax.rem(c, pairs)
        arrived(left.at[:, q, bp, :, :, :, lanes], recv_near.at[c if sem is None else sem])
        made = []
        for par in range(2):
            both = jnp.concatenate([
                left[p, q, bp, par, :, :, lanes].reshape(depth, lanes.size) for p in range(2)
            ], axis=0)
            made.append(jnp.dot(first_mat[...], both, preferred_element_type=jnp.float32))
        for p in range(2):
            parts = [m[p * depth:(p + 1) * depth].reshape(groups, HALF, lanes.size) for m in made]
            mixed = jnp.concatenate(parts, axis=1).astype(jnp.bfloat16)
            right[p, q, bp, :, :, :, lanes] = mixed.reshape(2, sixteens, TILE, lanes.size)
        far_start(c, 0, False, lanes)
        far_start(c, 1, False, lanes)

    def last_chunk(c, lanes=every_lane):
        q, bp = lax.div(c, pairs), lax.rem(c, pairs)
        wide = [
            left[p, q, bp, :, :, :, lanes].reshape(groups, TILE, lanes.size).astype(jnp.float32) for p in range(2)
        ]
        for par in range(2):
            both = jnp.concatenate([
                w[:, par * HALF:(par + 1) * HALF].reshape(depth, lanes.size).astype(jnp.bfloat16) for w in wide
            ], axis=0)
            made = jnp.dot(first_mat[...], both, preferred_element_type=jnp.float32)
            for p in range(2):
                part = made[p * depth:(p + 1) * depth].reshape(sixteens, TILE, lanes.size)
                right[p, q, bp, par, :, :, lanes] = part.astype(jnp.bfloat16)
        for d in near_order:
            home_start(q, bp, d, lanes)

    def finish_chunk(q):
        arrived(upper.at[:, pl.ds(q * TILE, TILE)], recv_home.at[q])

        @pl.when(q < chunks - 1)
        def _():
            def group(g, carry):
                for p in range(2):
                    rows = upper[p, pl.ds(q * TILE, TILE), g].astype(jnp.float32)
                    upper[p, pl.ds(q * TILE, TILE), g] = jnp.swapaxes(rows, 0, 1).astype(jnp.bfloat16)
                return carry

            lax.fori_loop(0, a_tiles, group, 0)

    def near_all(q):
        for bp in range(pairs - 1):
            for d in near_order:
                near_start(q, bp, d)

        @pl.when(q < chunks - 1)
        def _():
            for d in near_order:
                near_start(q, pairs - 1, d)

        @pl.when(q == chunks - 1)
        def _():
            for s in range(sheets):
                for d in near_order:
                    near_start(q, pairs - 1, d, lanes=sheet[s], sem=spare(last - 1, s))

    start = jnp.int32(0)
    early = a_tiles // 2
    kick_chunk(start, 0, early)
    pl.semaphore_wait(barrier, devices - 1)
    for d in near_order:
        near_start(start, 0, d, 0, early, sheet[0], spare(start, 0))
    kick_chunk(start, early)
    for d in near_order:
        near_start(start, 0, d, early, early, sheet[0], spare(start, 0))
    for s in range(1, sheets):
        for d in near_order:
            near_start(start, 0, d, lanes=sheet[s], sem=spare(start, s))
    for bp in range(1, pairs):
        for d in near_order:
            near_start(start, bp, d)

    def rad_copy(n):
        to = flip(at_b, n, bits_b)
        return pltpu.make_async_remote_copy(
            src_ref=radial_ref.at[:, pl.ds(pl.multiple_of(to * TILE, TILE), TILE)], dst_ref=far.at[at_b],
            send_sem=rad_send, recv_sem=rad_recv, device_id=(at_a, to), device_id_type=MESH,
        )

    pltpu.make_async_copy(
        radial_ref.at[:, pl.ds(pl.multiple_of(at_b * TILE, TILE), TILE)], far.at[at_b], rad_recv
    ).start()

    def rad_start(n, carry):
        rad_copy(n).start()
        return carry

    lax.fori_loop(1, rb, rad_start, 0)

    for source, target in ((first_ref, first_mat), (second_ref, second_mat)):
        target[:depth, :depth] = source[0]
        target[depth:, depth:] = source[0]
        target[:depth, depth:] = -source[1]
        target[depth:, :depth] = source[1]

    def opening(t, carry):
        @pl.when(t < chunks)
        def _():
            kick_chunk(t)
            near_all(t)

        def one(c, carry):
            @pl.when(edge(c))
            def _():
                for s in range(sheets):
                    first_chunk(c, sheet[s], spare(c, s))

            @pl.when(jnp.logical_not(edge(c)))
            def _():
                first_chunk(c)

            return carry

        lax.fori_loop((t - 1) * pairs, t * pairs, one, 0)
        return carry

    lax.fori_loop(1, chunks + 1, opening, 0)
    def crossing(c, h):
        far_start(c, h, True)
        return h

    lax.fori_loop(0, chunks * pairs, crossing, 0)
    lax.fori_loop(0, FAR_LEAD, crossing, 1)

    arrived(lower.at[:, 0:lower.shape[1] * (ra - 1) // ra], send_sem.at[0])
    arrived(far, rad_recv)

    width = LANES
    block = a_tiles * TILE

    def middle(h, carry):
        arrived(upper.at[:, pl.ds(h * halfway, halfway)], recv_far.at[h])

        @pl.when(h == 0)
        def _():
            lax.fori_loop(FAR_LEAD, chunks * pairs, crossing, 1)

        pieces = far[:, :, pl.ds(pl.multiple_of(h * HALF, HALF), HALF)].reshape(rb * KTERMS, HALF, b_rows)
        lines[...] = jnp.swapaxes(pieces, 0, 1)

        def spread(m, carry):
            for p in range(2):
                wide = upper[p, h * halfway + m].astype(jnp.float32).reshape(block, channels)
                for s in range(sheets):
                    turn[p, s, pl.ds(pl.multiple_of(m * block, block), block)] = wide[:, s * width:(s + 1) * width]
            return carry

        lax.fori_loop(0, halfway, spread, 0)

        def line(a, carry):
            size = second_ref.shape[1]
            at = pl.ds(a, size, stride=HALF)
            both = jnp.concatenate([
                jnp.concatenate([turn[p, s, at] for s in range(sheets)], axis=1).astype(jnp.bfloat16) for p in range(2)
            ], axis=0)
            made = jnp.dot(second_mat[...], both, preferred_element_type=jnp.float32).astype(jnp.bfloat16)
            laid = jnp.transpose(lines[a])

            def factor_of(k):
                return jnp.concatenate([
                    jnp.broadcast_to(laid[:, n * KTERMS + k:n * KTERMS + k + 1], (b_rows, channels)) for n in range(rb)
                ], axis=0)

            kicked = kick([made[:size], made[size:]], factor_of, size)
            both = jnp.concatenate([x.astype(jnp.bfloat16) for x in kicked], axis=0)
            made = jnp.dot(second_mat[...], both, preferred_element_type=jnp.float32)
            for p in range(2):
                for s in range(sheets):
                    turn[p, s, at] = made[p * size:(p + 1) * size, s * width:(s + 1) * width]
            return carry

        lax.fori_loop(0, HALF, line, 0)

        def gather(m, carry):
            for p in range(2):
                wide = jnp.concatenate([
                    turn[p, s, pl.ds(pl.multiple_of(m * block, block), block)] for s in range(sheets)
                ], axis=1)
                lower[p, h * halfway + m] = wide.astype(jnp.bfloat16).reshape(a_tiles, TILE, channels)
            return carry

        lax.fori_loop(0, halfway, gather, 0)

        every(lambda c: back_start(c, h, True))
        return carry

    lax.fori_loop(0, 2, middle, 0)

    def part(c, s):
        @pl.when(edge(c))
        def _():
            for h in range(2):
                back_start(c, h, False, sheet[s], spare(c, s))

        @pl.when(jnp.logical_not(edge(c)))
        def _():
            back_start(c, s, False)

    part(jnp.int32(0), 0)
    part(jnp.int32(0), 1)
    part(jnp.int32(1), 0)
    arrived(right.at[:, :, :, :, 0:sixteens * (devices - 1) // devices], send_sem.at[1])

    def closing(t, carry):
        @pl.when(t < chunks)
        def _():
            def one(c, carry):
                bp = lax.rem(c, pairs)

                def onward():
                    @pl.when(c + 1 < last)
                    def _():
                        part(c + 1, 1)

                    @pl.when(c + 2 < last)
                    def _():
                        part(c + 2, 0)

                @pl.when(jnp.logical_not(edge(c)))
                def _():
                    arrived(left.at[:, t, bp], recv_back.at[c])
                    onward()
                    last_chunk(c)

                @pl.when(edge(c))
                def _():
                    arrived(left.at[:, t, bp, 0], recv_back.at[c])
                    for s in range(sheets):
                        arrived(left.at[:, t, bp, 0, :, :, sheet[s]], recv_back.at[spare(c, s)])
                        if s == sheets - 1:
                            onward()
                        last_chunk(c, sheet[s])

                return carry

            lax.fori_loop(t * pairs, (t + 1) * pairs, one, 0)

        @pl.when(t >= 1)
        def _():
            finish_chunk(t - 1)

        return carry

    lax.fori_loop(0, chunks + 1, closing, 0)

    arrived(lower.at[:, 0:lower.shape[1] * (devices - 1) // devices], send_sem.at[2])
    arrived(right.at[:, :, :, :, 0:sixteens * (ra - 1) // ra], send_sem.at[3])
    arrived(far.at[0:rb - 1], rad_send)


def unfold_kernel(in_ref, out_ref, stage, sem):
    tiles = stage.shape[1] // TILE
    done = in_ref.shape[1] // TILE - 1

    def ready(n, carry):
        q, g = lax.div(n, tiles), lax.rem(n, tiles)
        at = pl.ds(pl.multiple_of(q * TILE, TILE), TILE)
        pltpu.make_async_copy(in_ref.at[:, at, g], out_ref.at[:, pl.ds(g * TILE, TILE), at], sem).start()
        return carry

    lax.fori_loop(0, done * tiles, ready, 0)
    at = pl.ds(done * TILE, TILE)

    def group(g, carry):
        span = pl.ds(g * TILE, TILE)
        for p in range(2):
            turned = jnp.swapaxes(in_ref[p, at, g].astype(jnp.float32), 0, 1)
            stage[p, span] = turned.astype(jnp.bfloat16)
        pltpu.make_async_copy(stage.at[:, span], out_ref.at[:, span, at], sem).start()
        return carry

    lax.fori_loop(0, tiles, group, 0)
    pltpu.make_async_copy(in_ref, in_ref, sem).wait()


def unfold(folded, shape):
    return pl.pallas_call(
        unfold_kernel,
        in_specs=[pl.BlockSpec(memory_space=pltpu.VMEM)],
        out_specs=pl.BlockSpec(memory_space=pl.ANY),
        out_shape=jax.ShapeDtypeStruct(shape, jnp.bfloat16),
        scratch_shapes=[
            pltpu.VMEM((2, shape[1], TILE, shape[3]), jnp.bfloat16),
            pltpu.SemaphoreType.DMA(()),
        ],
        compiler_params=pltpu.CompilerParams(vmem_limit_bytes=16 * 2**20),
    )(folded)


def on_device(amplitude, coupling, pattern, radial, first_prop, second_prop):
    a_rows, b_rows, channels = amplitude.shape[1:]
    n_a, n_b = first_prop.shape[1], second_prop.shape[1]
    ra, rb = lax.axis_size("ra"), lax.axis_size("rb")
    devices = ra * rb
    chunks = b_rows // TILE
    fits = (
        channels == 2 * LANES and ra & (ra - 1) == 0 and rb == HALF and ra in (2, 4) and n_a == n_b
        and n_a == TILE * devices and n_b == TILE * devices and a_rows % TILE == 0 and b_rows % TILE == 0
        and chunks % 2 == 0 and chunks == ra and a_rows == TILE * HALF and b_rows <= LANES
    )
    if not fits:
        return plain(amplitude, coupling, pattern, radial, first_prop, second_prop)

    pairs = TILE // ra // 2
    groups = n_a // HALF
    flat = (2, chunks * TILE, a_rows // TILE, TILE, channels)
    tall = (2, chunks, pairs, 2, groups // 2, TILE, channels)
    whole = pl.BlockSpec(memory_space=pltpu.VMEM)
    kept = pl.BlockSpec(memory_space=pl.ANY)
    dma = pltpu.SemaphoreType.DMA
    folded = pl.pallas_call(
        functools.partial(fused_kernel, ra, rb),
        in_specs=[kept, whole, pl.BlockSpec(memory_space=pltpu.SMEM), whole, whole, whole],
        out_specs=whole,
        out_shape=pltpu.VMEM(flat, jnp.bfloat16),
        scratch_shapes=[
            pltpu.VMEM(flat, jnp.bfloat16),
            pltpu.VMEM(tall, jnp.bfloat16),
            pltpu.VMEM(tall, jnp.bfloat16),
            pltpu.VMEM((2, channels // LANES, n_b * HALF, LANES), jnp.float32),
            pltpu.VMEM((2, 2, a_rows, TILE, channels), jnp.bfloat16),
            pltpu.VMEM((2 * n_a, 2 * n_a), jnp.bfloat16),
            pltpu.VMEM((2 * n_b, 2 * n_b), jnp.bfloat16),
            pltpu.VMEM((KTERMS, channels, channels), jnp.bfloat16),
            pltpu.VMEM((KTERMS, a_rows, b_rows), jnp.float32),
            pltpu.VMEM((a_rows // HALF, b_rows, KTERMS * HALF), jnp.float32),
            pltpu.VMEM((rb, KTERMS, TILE, b_rows), jnp.float32),
            pltpu.VMEM((HALF, rb * KTERMS, b_rows), jnp.float32),
            dma((2,)), dma((4,)), dma((chunks * pairs + 2 * channels // LANES,)), dma((2,)),
            dma((chunks * pairs + 2 * channels // LANES,)), dma((chunks,)),
            dma(()), dma(()),
        ],
        compiler_params=pltpu.CompilerParams(
            collective_id=0, has_side_effects=True, vmem_limit_bytes=55 * 2**20
        ),
    )(amplitude, coupling, pattern.transpose(1, 2, 0), radial.transpose(0, 2, 1), first_prop, second_prop)
    return unfold(folded, amplitude.shape)


def solution(mesh):
    return jax.shard_map(
        on_device,
        mesh=mesh,
        in_specs=(P(None, "ra", "rb", None), P(), P(), P(None, "ra", "rb"), P(), P()),
        out_specs=P(None, "ra", "rb", None),
        check_vma=False,
    )
```

```python
import functools

import jax
import jax.numpy as jnp
from jax import lax
from jax.experimental import pallas as pl
from jax.experimental.pallas import tpu as pltpu
from jax.sharding import PartitionSpec as P

KTERMS = 6
STEPS = 2
LANES = 128
TILE = 16
HALF = 8
MESH = pl.DeviceIdType.MESH


def complex_rows(matrix, piece):
    form = "ac,cqw->aqw"
    real_part = jnp.einsum(
        form, matrix[0], piece[0], preferred_element_type=jnp.float32
    ) - jnp.einsum(form, matrix[1], piece[1], preferred_element_type=jnp.float32)
    imag_part = jnp.einsum(
        form, matrix[0], piece[1], preferred_element_type=jnp.float32
    ) + jnp.einsum(form, matrix[1], piece[0], preferred_element_type=jnp.float32)
    return jnp.stack([real_part, imag_part]).astype(jnp.bfloat16)


def masked_weights(coupling, pattern):
    channels = coupling.shape[1]
    count = pattern.shape[1]
    block_size = channels // count
    spread = jnp.broadcast_to(
        pattern[:, :, None, :, None], (KTERMS, count, block_size, count, block_size)
    )
    return coupling * spread.reshape(KTERMS, channels, channels).astype(jnp.bfloat16)


def plain(amplitude, coupling, pattern, radial, first_prop, second_prop):
    first_rows, second_rows, channels = (amplitude.shape[1], amplitude.shape[2], amplitude.shape[3])
    cells = first_rows * second_rows
    groups_a = lax.axis_size("ra")
    groups_b = lax.axis_size("rb")
    width_a = channels // groups_a
    width_b = channels // groups_b
    weights = masked_weights(coupling, pattern)
    radial_cells = radial.reshape(KTERMS, cells).T
    for sweep in range(STEPS):
        flat = amplitude.reshape(2 * cells, channels)
        applied = jnp.einsum("mj,kij->mki", flat, weights, preferred_element_type=jnp.float32)
        applied = applied.reshape(2, cells, KTERMS, channels)
        coupled = jnp.sum(applied * radial_cells[None, :, :, None], axis=2)
        wide = amplitude.reshape(2, cells, channels).astype(jnp.float32)
        kicked = jnp.stack([wide[0] + coupled[1], wide[1] - coupled[0]]).astype(jnp.bfloat16)
        grouped = kicked.reshape(2, first_rows, second_rows, groups_a, width_a)
        grouped = grouped.transpose(0, 1, 3, 2, 4).reshape(
            2, first_rows, groups_a, second_rows * width_a
        )
        half = complex_rows(
            first_prop, lax.all_to_all(grouped, "ra", split_axis=2, concat_axis=1, tiled=True)
        )
        restored = lax.all_to_all(half, "ra", split_axis=1, concat_axis=2, tiled=True)
        restored = restored.reshape(2, first_rows, groups_a, second_rows, width_a)
        restored = restored.transpose(0, 1, 3, 2, 4).reshape(
            2, first_rows, second_rows, groups_b, width_b
        )
        regrouped = restored.transpose(0, 2, 3, 1, 4).reshape(
            2, second_rows, groups_b, first_rows * width_b
        )
        moved = complex_rows(
            second_prop, lax.all_to_all(regrouped, "rb", split_axis=2, concat_axis=1, tiled=True)
        )
        settled = lax.all_to_all(moved, "rb", split_axis=1, concat_axis=2, tiled=True)
        settled = settled.reshape(2, second_rows, groups_b, first_rows, width_b)
        amplitude = settled.transpose(0, 3, 1, 2, 4).reshape(2, first_rows, second_rows, channels)
    return amplitude


FAR_LEAD = 3


def flip(value, mask, bits):
    out = 0
    for n in range(bits):
        weight = 1 << n
        out = out + lax.rem(lax.div(value, weight) + lax.div(mask, weight), 2) * weight
    return out


def fused_kernel(ra, rb, amp_ref, coupling_ref, pattern_ref, turned_ref, first_ref, second_ref, upper,
                 lower, left, right, turn, stage, first_mat, second_mat, weights_ref, radial_ref, near, far, lines,
                 load_sem, send_sem, recv_near, recv_far, recv_back, recv_home, rad_send, rad_recv):
    at_a, at_b = lax.axis_index("ra"), lax.axis_index("rb")
    bits_a, bits_b = ra.bit_length() - 1, rb.bit_length() - 1
    chunks = left.shape[1]
    pairs = left.shape[2]
    sixteens = left.shape[4]
    groups = 2 * sixteens
    per = pairs * 2
    depth = first_ref.shape[1]
    halfway = lower.shape[1] // 2
    channels = lower.shape[4]
    a_tiles = lower.shape[2]
    devices = ra * rb
    route = [("b", bits_b - 1)] + [("b", n) for n in range(bits_b - 1)]
    route = route + [("a", n) for n in range(bits_a)]

    def partner(d):
        mask_a, mask_b = 0, 0
        for n, (axis, bit) in enumerate(route):
            one = lax.rem(lax.div(d, 1 << n), 2) * (1 << bit)
            if axis == "a":
                mask_a = mask_a + one
            else:
                mask_b = mask_b + one
        return flip(at_a, mask_a, bits_a), flip(at_b, mask_b, bits_b)

    barrier = pltpu.get_barrier_semaphore()

    def greet(d, carry):
        to_a, to_b = partner(devices - d)
        pl.semaphore_signal(barrier, inc=1, device_id=(to_a, to_b), device_id_type=MESH)
        return carry

    lax.fori_loop(1, devices, greet, 0)

    every_lane = pl.ds(0, channels)
    sheets = channels // LANES
    sheet = [pl.ds(s * LANES, LANES) for s in range(sheets)]
    last = chunks * pairs

    def edge(c):
        return (c == 0) | (c == last - 1)

    def spare(c, s):
        return last + lax.div(c, last - 1) * sheets + s

    def load(q):
        slot = lax.rem(q, 2)
        return pltpu.make_async_copy(amp_ref.at[:, :, pl.ds(q * TILE, TILE)], stage.at[slot], load_sem.at[slot])

    load(jnp.int32(0)).start()
    load(jnp.int32(1)).start()

    b_rows = amp_ref.shape[2]
    blocks = pattern_ref.shape[0]
    size_block = channels // blocks
    lane = lax.broadcasted_iota(jnp.int32, (size_block, channels), 1)
    for k in range(KTERMS):
        masked = []
        for i in range(blocks):
            keep = jnp.zeros((size_block, channels), jnp.float32)
            for j in range(blocks):
                inside = (lane >= j * size_block) & (lane < (j + 1) * size_block)
                keep = jnp.where(inside, pattern_ref[i, j, k].astype(jnp.float32), keep)
            masked.append(coupling_ref[k, i * size_block:(i + 1) * size_block].astype(jnp.float32) * keep)
        weights_ref[k] = jnp.transpose(jnp.concatenate(masked, axis=0)).astype(jnp.bfloat16)

    duos = KTERMS // 2
    for m in range(duos):
        radial_ref[m] = jnp.transpose(turned_ref[2 * m:2 * m + 2].reshape(2 * b_rows, radial_ref.shape[1]))

    def lay(g, carry):
        at = pl.ds(pl.multiple_of(g * HALF, HALF), HALF)
        near[g] = jnp.transpose(radial_ref[:, at].reshape(duos * HALF, 2 * b_rows))
        return carry

    lax.fori_loop(0, radial_ref.shape[1] // HALF, lay, 0)

    def kick(planes, factor_of, count):
        both = jnp.concatenate(planes, axis=0)
        total = [None, None]
        for k in range(KTERMS):
            applied = jnp.dot(both, weights_ref[k], preferred_element_type=jnp.float32)
            factor = factor_of(k)
            for p in range(2):
                term = applied[p * count:(p + 1) * count] * factor
                total[p] = term if k == 0 else total[p] + term
        return planes[0].astype(jnp.float32) + total[1], planes[1].astype(jnp.float32) - total[0]

    def kick_chunk(q, first=0, stop=None):
        slot = lax.rem(q, 2)
        if first == 0:
            load(q).wait()

        def group(g, carry):
            count = TILE * TILE
            planes = [stage[slot, p, pl.ds(g * TILE, TILE)].reshape(count, channels) for p in range(2)]
            laid = [[
                near[g * 2 + n, pl.ds(pl.multiple_of(odd * b_rows + q * TILE, TILE), TILE)] for n in range(2)
            ] for odd in range(2)]

            def factor_of(k):
                m, odd = divmod(k, 2)
                return jnp.concatenate([
                    jnp.broadcast_to(
                        laid[odd][n // HALF][:, m * HALF + n % HALF:m * HALF + n % HALF + 1], (TILE, channels)
                    ) for n in range(TILE)
                ], axis=0)

            result = kick(planes, factor_of, count)
            for p in range(2):
                turned = jnp.swapaxes(result[p].reshape(TILE, TILE, channels), 0, 1).astype(jnp.bfloat16)
                lower[p, pl.ds(q * TILE, TILE), g] = turned
            return carry

        lax.fori_loop(first, a_tiles if stop is None else stop, group, 0)
        if stop is None:
            @pl.when(q + 2 < chunks)
            def _():
                load(q + 2).start()

    def near_start(q, bp, d, first=0, count=None, lanes=every_lane, sem=None):
        to = flip(at_a, d, bits_a) if d < ra // 2 else opposite + d - ra // 2
        count = a_tiles if count is None else count
        source = lower.at[:, pl.ds(q * TILE + to * per + bp * 2, 2), pl.ds(first, count), :, lanes]
        target = left.at[:, q, bp, :, pl.ds(at_a * a_tiles + first, count), :, lanes]
        sem = recv_near.at[q * pairs + bp if sem is None else sem]
        if d == 0:
            pltpu.make_async_copy(source, target, sem).start()
        else:
            pltpu.make_async_remote_copy(
                src_ref=source, dst_ref=target, send_sem=send_sem.at[0], recv_sem=sem,
                device_id=(to, at_b), device_id_type=MESH,
            ).start()

    def home_start(q, bp, d, lanes=every_lane):
        to = flip(at_a, d, bits_a)
        source = right.at[:, q, bp, :, pl.ds(to * a_tiles, a_tiles), :, lanes]
        target = upper.at[:, pl.ds(q * TILE + at_a * per + bp * 2, 2), :, :, lanes]
        if d == 0:
            pltpu.make_async_copy(source, target, recv_home.at[q]).start()
        else:
            pltpu.make_async_remote_copy(
                src_ref=source, dst_ref=target, send_sem=send_sem.at[3], recv_sem=recv_home.at[q],
                device_id=(to, at_b), device_id_type=MESH,
            ).start()

    opposite = (1 - lax.div(at_a, ra // 2)) * (ra // 2)
    near_order = list(range(ra // 2, ra)) + list(range(1, ra // 2)) + [0]
    side = devices // 2

    def place(i, j, h):
        index = (i * rb + j) * 2 + h
        return lax.div(index, sixteens), lax.rem(index, sixteens)

    def far_start(c, h, crossing, lanes=every_lane):
        q, bp = lax.div(c, pairs), lax.rem(c, pairs)
        row = h * halfway + at_b * chunks + q
        target = upper.at[:, row, at_a * pairs + bp, :, lanes]

        def one(d, carry):
            to_a, to_b = partner(d)
            high, low = place(to_a, to_b, h)
            pltpu.make_async_remote_copy(
                src_ref=right.at[:, q, bp, high, low, :, lanes], dst_ref=target,
                send_sem=send_sem.at[1], recv_sem=recv_far.at[h], device_id=(to_a, to_b), device_id_type=MESH,
            ).start()
            return carry

        if crossing:
            lax.fori_loop(side, devices, one, 0)
        else:
            lax.fori_loop(1, side, one, 0)
            high, low = place(at_a, at_b, h)
            pltpu.make_async_copy(right.at[:, q, bp, high, low, :, lanes], target, recv_far.at[h]).start()

    def back_start(c, h, crossing, lanes=every_lane, sem=None):
        q, bp = lax.div(c, pairs), lax.rem(c, pairs)
        high, low = place(at_a, at_b, h)
        target = left.at[:, q, bp, high, low, :, lanes]
        sem = recv_back.at[c if sem is None else sem]

        def one(d, carry):
            to_a, to_b = partner(d)
            pltpu.make_async_remote_copy(
                src_ref=lower.at[:, h * halfway + to_b * chunks + q, to_a * pairs + bp, :, lanes], dst_ref=target,
                send_sem=send_sem.at[2], recv_sem=sem, device_id=(to_a, to_b), device_id_type=MESH,
            ).start()
            return carry

        if crossing:
            lax.fori_loop(side, devices, one, 0)
        else:
            lax.fori_loop(1, side, one, 0)
            pltpu.make_async_copy(
                lower.at[:, h * halfway + at_b * chunks + q, at_a * pairs + bp, :, lanes], target, sem
            ).start()

    def every(action):
        def one(c, carry):
            action(c)
            return carry

        lax.fori_loop(0, chunks * pairs, one, 0)

    def arrived(ref, sem):
        pltpu.make_async_copy(ref, ref, sem).wait()

    def first_chunk(c, lanes=every_lane, sem=None):
        q, bp = lax.div(c, pairs), lax.rem(c, pairs)
        arrived(left.at[:, q, bp, :, :, :, lanes], recv_near.at[c if sem is None else sem])
        made = []
        for par in range(2):
            both = jnp.concatenate([
                left[p, q, bp, par, :, :, lanes].reshape(depth, lanes.size) for p in range(2)
            ], axis=0)
            made.append(jnp.dot(first_mat[...], both, preferred_element_type=jnp.float32))
        for p in range(2):
            parts = [m[p * depth:(p + 1) * depth].reshape(groups, HALF, lanes.size) for m in made]
            mixed = jnp.concatenate(parts, axis=1).astype(jnp.bfloat16)
            right[p, q, bp, :, :, :, lanes] = mixed.reshape(2, sixteens, TILE, lanes.size)
        far_start(c, 0, False, lanes)
        far_start(c, 1, False, lanes)

    def last_chunk(c, lanes=every_lane):
        q, bp = lax.div(c, pairs), lax.rem(c, pairs)
        wide = [
            left[p, q, bp, :, :, :, lanes].reshape(groups, TILE, lanes.size).astype(jnp.float32) for p in range(2)
        ]
        for par in range(2):
            both = jnp.concatenate([
                w[:, par * HALF:(par + 1) * HALF].reshape(depth, lanes.size).astype(jnp.bfloat16) for w in wide
            ], axis=0)
            made = jnp.dot(first_mat[...], both, preferred_element_type=jnp.float32)
            for p in range(2):
                part = made[p * depth:(p + 1) * depth].reshape(sixteens, TILE, lanes.size)
                right[p, q, bp, par, :, :, lanes] = part.astype(jnp.bfloat16)
        for d in near_order:
            home_start(q, bp, d, lanes)

    def finish_chunk(q):
        arrived(upper.at[:, pl.ds(q * TILE, TILE)], recv_home.at[q])

        @pl.when(q < chunks - 1)
        def _():
            def group(g, carry):
                for p in range(2):
                    rows = upper[p, pl.ds(q * TILE, TILE), g].astype(jnp.float32)
                    upper[p, pl.ds(q * TILE, TILE), g] = jnp.swapaxes(rows, 0, 1).astype(jnp.bfloat16)
                return carry

            lax.fori_loop(0, a_tiles, group, 0)

    def near_all(q):
        for bp in range(pairs - 1):
            for d in near_order:
                near_start(q, bp, d)

        @pl.when(q < chunks - 1)
        def _():
            for d in near_order:
                near_start(q, pairs - 1, d)

        @pl.when(q == chunks - 1)
        def _():
            for s in range(sheets):
                for d in near_order:
                    near_start(q, pairs - 1, d, lanes=sheet[s], sem=spare(last - 1, s))

    start = jnp.int32(0)
    early = a_tiles // 2
    kick_chunk(start, 0, early)
    pl.semaphore_wait(barrier, devices - 1)
    for d in near_order:
        near_start(start, 0, d, 0, early, sheet[0], spare(start, 0))
    kick_chunk(start, early)
    for d in near_order:
        near_start(start, 0, d, early, early, sheet[0], spare(start, 0))
    for s in range(1, sheets):
        for d in near_order:
            near_start(start, 0, d, lanes=sheet[s], sem=spare(start, s))
    for bp in range(1, pairs):
        for d in near_order:
            near_start(start, bp, d)

    def rad_copy(n):
        to = flip(at_b, n, bits_b)
        return pltpu.make_async_remote_copy(
            src_ref=radial_ref.at[:, pl.ds(pl.multiple_of(to * TILE, TILE), TILE)], dst_ref=far.at[at_b],
            send_sem=rad_send, recv_sem=rad_recv, device_id=(at_a, to), device_id_type=MESH,
        )

    pltpu.make_async_copy(
        radial_ref.at[:, pl.ds(pl.multiple_of(at_b * TILE, TILE), TILE)], far.at[at_b], rad_recv
    ).start()

    def rad_start(n, carry):
        rad_copy(n).start()
        return carry

    lax.fori_loop(1, rb, rad_start, 0)

    for source, target in ((first_ref, first_mat), (second_ref, second_mat)):
        target[:depth, :depth] = source[0]
        target[depth:, depth:] = source[0]
        target[:depth, depth:] = -source[1]
        target[depth:, :depth] = source[1]

    def opening(t, carry):
        @pl.when(t < chunks)
        def _():
            kick_chunk(t)
            near_all(t)

        def one(c, carry):
            @pl.when(edge(c))
            def _():
                for s in range(sheets):
                    first_chunk(c, sheet[s], spare(c, s))

            @pl.when(jnp.logical_not(edge(c)))
            def _():
                first_chunk(c)

            return carry

        lax.fori_loop((t - 1) * pairs, t * pairs, one, 0)
        return carry

    lax.fori_loop(1, chunks + 1, opening, 0)
    def crossing(c, h):
        far_start(c, h, True)
        return h

    lax.fori_loop(0, chunks * pairs, crossing, 0)
    lax.fori_loop(0, FAR_LEAD, crossing, 1)

    arrived(lower.at[:, 0:lower.shape[1] * (ra - 1) // ra], send_sem.at[0])
    arrived(far, rad_recv)

    width = LANES
    block = a_tiles * TILE

    def middle(h, carry):
        arrived(upper.at[:, pl.ds(h * halfway, halfway)], recv_far.at[h])

        @pl.when(h == 0)
        def _():
            lax.fori_loop(FAR_LEAD, chunks * pairs, crossing, 1)

        pieces = far[:, :, pl.ds(pl.multiple_of(h * HALF, HALF), HALF)].reshape(rb * duos, HALF, 2 * b_rows)
        lines[...] = jnp.swapaxes(pieces, 0, 1)

        def spread(m, carry):
            for p in range(2):
                wide = upper[p, h * halfway + m].astype(jnp.float32).reshape(block, channels)
                for s in range(sheets):
                    turn[p, s, pl.ds(pl.multiple_of(m * block, block), block)] = wide[:, s * width:(s + 1) * width]
            return carry

        lax.fori_loop(0, halfway, spread, 0)

        def line(a, carry):
            size = second_ref.shape[1]
            at = pl.ds(a, size, stride=HALF)
            both = jnp.concatenate([
                jnp.concatenate([turn[p, s, at] for s in range(sheets)], axis=1).astype(jnp.bfloat16) for p in range(2)
            ], axis=0)
            made = jnp.dot(second_mat[...], both, preferred_element_type=jnp.float32).astype(jnp.bfloat16)
            laid = jnp.transpose(lines[a])

            def factor_of(k):
                m, odd = divmod(k, 2)
                half = laid[odd * b_rows:(odd + 1) * b_rows]
                return jnp.concatenate([
                    jnp.broadcast_to(half[:, n * duos + m:n * duos + m + 1], (b_rows, channels)) for n in range(rb)
                ], axis=0)

            kicked = kick([made[:size], made[size:]], factor_of, size)
            both = jnp.concatenate([x.astype(jnp.bfloat16) for x in kicked], axis=0)
            made = jnp.dot(second_mat[...], both, preferred_element_type=jnp.float32)
            for p in range(2):
                for s in range(sheets):
                    turn[p, s, at] = made[p * size:(p + 1) * size, s * width:(s + 1) * width]
            return carry

        lax.fori_loop(0, HALF, line, 0)

        def gather(m, carry):
            for p in range(2):
                wide = jnp.concatenate([
                    turn[p, s, pl.ds(pl.multiple_of(m * block, block), block)] for s in range(sheets)
                ], axis=1)
                lower[p, h * halfway + m] = wide.astype(jnp.bfloat16).reshape(a_tiles, TILE, channels)
            return carry

        lax.fori_loop(0, halfway, gather, 0)

        every(lambda c: back_start(c, h, True))
        return carry

    lax.fori_loop(0, 2, middle, 0)

    def part(c, s):
        @pl.when(edge(c))
        def _():
            for h in range(2):
                back_start(c, h, False, sheet[s], spare(c, s))

        @pl.when(jnp.logical_not(edge(c)))
        def _():
            back_start(c, s, False)

    part(jnp.int32(0), 0)
    part(jnp.int32(0), 1)
    part(jnp.int32(1), 0)
    arrived(right.at[:, :, :, :, 0:sixteens * (devices - 1) // devices], send_sem.at[1])

    def closing(t, carry):
        @pl.when(t < chunks)
        def _():
            def one(c, carry):
                bp = lax.rem(c, pairs)

                def onward():
                    @pl.when(c + 1 < last)
                    def _():
                        part(c + 1, 1)

                    @pl.when(c + 2 < last)
                    def _():
                        part(c + 2, 0)

                @pl.when(jnp.logical_not(edge(c)))
                def _():
                    arrived(left.at[:, t, bp], recv_back.at[c])
                    onward()
                    last_chunk(c)

                @pl.when(edge(c))
                def _():
                    arrived(left.at[:, t, bp, 0], recv_back.at[c])
                    for s in range(sheets):
                        arrived(left.at[:, t, bp, 0, :, :, sheet[s]], recv_back.at[spare(c, s)])
                        if s == sheets - 1:
                            onward()
                        last_chunk(c, sheet[s])

                return carry

            lax.fori_loop(t * pairs, (t + 1) * pairs, one, 0)

        @pl.when(t >= 1)
        def _():
            finish_chunk(t - 1)

        return carry

    lax.fori_loop(0, chunks + 1, closing, 0)

    arrived(lower.at[:, 0:lower.shape[1] * (devices - 1) // devices], send_sem.at[2])
    arrived(right.at[:, :, :, :, 0:sixteens * (ra - 1) // ra], send_sem.at[3])
    arrived(far.at[0:rb - 1], rad_send)


def unfold_kernel(in_ref, out_ref, stage, sem):
    tiles = stage.shape[1] // TILE
    done = in_ref.shape[1] // TILE - 1

    def ready(n, carry):
        q, g = lax.div(n, tiles), lax.rem(n, tiles)
        at = pl.ds(pl.multiple_of(q * TILE, TILE), TILE)
        pltpu.make_async_copy(in_ref.at[:, at, g], out_ref.at[:, pl.ds(g * TILE, TILE), at], sem).start()
        return carry

    lax.fori_loop(0, done * tiles, ready, 0)
    at = pl.ds(done * TILE, TILE)

    def group(g, carry):
        span = pl.ds(g * TILE, TILE)
        for p in range(2):
            turned = jnp.swapaxes(in_ref[p, at, g].astype(jnp.float32), 0, 1)
            stage[p, span] = turned.astype(jnp.bfloat16)
        pltpu.make_async_copy(stage.at[:, span], out_ref.at[:, span, at], sem).start()
        return carry

    lax.fori_loop(0, tiles, group, 0)
    pltpu.make_async_copy(in_ref, in_ref, sem).wait()


def unfold(folded, shape):
    return pl.pallas_call(
        unfold_kernel,
        in_specs=[pl.BlockSpec(memory_space=pltpu.VMEM)],
        out_specs=pl.BlockSpec(memory_space=pl.ANY),
        out_shape=jax.ShapeDtypeStruct(shape, jnp.bfloat16),
        scratch_shapes=[
            pltpu.VMEM((2, shape[1], TILE, shape[3]), jnp.bfloat16),
            pltpu.SemaphoreType.DMA(()),
        ],
        compiler_params=pltpu.CompilerParams(vmem_limit_bytes=16 * 2**20),
    )(folded)


def on_device(amplitude, coupling, pattern, radial, first_prop, second_prop):
    a_rows, b_rows, channels = amplitude.shape[1:]
    n_a, n_b = first_prop.shape[1], second_prop.shape[1]
    ra, rb = lax.axis_size("ra"), lax.axis_size("rb")
    devices = ra * rb
    chunks = b_rows // TILE
    fits = (
        channels == 2 * LANES and ra & (ra - 1) == 0 and rb == HALF and ra in (2, 4) and n_a == n_b
        and n_a == TILE * devices and n_b == TILE * devices and a_rows % TILE == 0 and b_rows % TILE == 0
        and chunks % 2 == 0 and chunks == ra and a_rows == TILE * HALF and 2 * b_rows == LANES and KTERMS % 2 == 0
    )
    if not fits:
        return plain(amplitude, coupling, pattern, radial, first_prop, second_prop)

    pairs = TILE // ra // 2
    groups = n_a // HALF
    flat = (2, chunks * TILE, a_rows // TILE, TILE, channels)
    tall = (2, chunks, pairs, 2, groups // 2, TILE, channels)
    whole = pl.BlockSpec(memory_space=pltpu.VMEM)
    kept = pl.BlockSpec(memory_space=pl.ANY)
    dma = pltpu.SemaphoreType.DMA
    folded = pl.pallas_call(
        functools.partial(fused_kernel, ra, rb),
        in_specs=[kept, whole, pl.BlockSpec(memory_space=pltpu.SMEM), whole, whole, whole],
        out_specs=whole,
        out_shape=pltpu.VMEM(flat, jnp.bfloat16),
        scratch_shapes=[
            pltpu.VMEM(flat, jnp.bfloat16),
            pltpu.VMEM(tall, jnp.bfloat16),
            pltpu.VMEM(tall, jnp.bfloat16),
            pltpu.VMEM((2, channels // LANES, n_b * HALF, LANES), jnp.float32),
            pltpu.VMEM((2, 2, a_rows, TILE, channels), jnp.bfloat16),
            pltpu.VMEM((2 * n_a, 2 * n_a), jnp.bfloat16),
            pltpu.VMEM((2 * n_b, 2 * n_b), jnp.bfloat16),
            pltpu.VMEM((KTERMS, channels, channels), jnp.bfloat16),
            pltpu.VMEM((KTERMS // 2, a_rows, 2 * b_rows), jnp.float32),
            pltpu.VMEM((a_rows // HALF, 2 * b_rows, KTERMS // 2 * HALF), jnp.float32),
            pltpu.VMEM((rb, KTERMS // 2, TILE, 2 * b_rows), jnp.float32),
            pltpu.VMEM((HALF, rb * KTERMS // 2, 2 * b_rows), jnp.float32),
            dma((2,)), dma((4,)), dma((chunks * pairs + 2 * channels // LANES,)), dma((2,)),
            dma((chunks * pairs + 2 * channels // LANES,)), dma((chunks,)),
            dma(()), dma(()),
        ],
        compiler_params=pltpu.CompilerParams(
            collective_id=0, has_side_effects=True, vmem_limit_bytes=55 * 2**20
        ),
    )(amplitude, coupling, pattern.transpose(1, 2, 0), radial.transpose(0, 2, 1), first_prop, second_prop)
    return unfold(folded, amplitude.shape)


def solution(mesh):
    return jax.shard_map(
        on_device,
        mesh=mesh,
        in_specs=(P(None, "ra", "rb", None), P(), P(), P(None, "ra", "rb"), P(), P()),
        out_specs=P(None, "ra", "rb", None),
        check_vma=False,
    )
```

```python
import functools

import jax
import jax.numpy as jnp
from jax import lax
from jax.experimental import pallas as pl
from jax.experimental.pallas import tpu as pltpu
from jax.sharding import PartitionSpec as P

KTERMS = 6
STEPS = 2
LANES = 128
TILE = 16
HALF = 8
MESH = pl.DeviceIdType.MESH


def complex_rows(matrix, piece):
    form = "ac,cqw->aqw"
    real_part = jnp.einsum(
        form, matrix[0], piece[0], preferred_element_type=jnp.float32
    ) - jnp.einsum(form, matrix[1], piece[1], preferred_element_type=jnp.float32)
    imag_part = jnp.einsum(
        form, matrix[0], piece[1], preferred_element_type=jnp.float32
    ) + jnp.einsum(form, matrix[1], piece[0], preferred_element_type=jnp.float32)
    return jnp.stack([real_part, imag_part]).astype(jnp.bfloat16)


def masked_weights(coupling, pattern):
    channels = coupling.shape[1]
    count = pattern.shape[1]
    block_size = channels // count
    spread = jnp.broadcast_to(
        pattern[:, :, None, :, None], (KTERMS, count, block_size, count, block_size)
    )
    return coupling * spread.reshape(KTERMS, channels, channels).astype(jnp.bfloat16)


def plain(amplitude, coupling, pattern, radial, first_prop, second_prop):
    first_rows, second_rows, channels = (amplitude.shape[1], amplitude.shape[2], amplitude.shape[3])
    cells = first_rows * second_rows
    groups_a = lax.axis_size("ra")
    groups_b = lax.axis_size("rb")
    width_a = channels // groups_a
    width_b = channels // groups_b
    weights = masked_weights(coupling, pattern)
    radial_cells = radial.reshape(KTERMS, cells).T
    for sweep in range(STEPS):
        flat = amplitude.reshape(2 * cells, channels)
        applied = jnp.einsum("mj,kij->mki", flat, weights, preferred_element_type=jnp.float32)
        applied = applied.reshape(2, cells, KTERMS, channels)
        coupled = jnp.sum(applied * radial_cells[None, :, :, None], axis=2)
        wide = amplitude.reshape(2, cells, channels).astype(jnp.float32)
        kicked = jnp.stack([wide[0] + coupled[1], wide[1] - coupled[0]]).astype(jnp.bfloat16)
        grouped = kicked.reshape(2, first_rows, second_rows, groups_a, width_a)
        grouped = grouped.transpose(0, 1, 3, 2, 4).reshape(
            2, first_rows, groups_a, second_rows * width_a
        )
        half = complex_rows(
            first_prop, lax.all_to_all(grouped, "ra", split_axis=2, concat_axis=1, tiled=True)
        )
        restored = lax.all_to_all(half, "ra", split_axis=1, concat_axis=2, tiled=True)
        restored = restored.reshape(2, first_rows, groups_a, second_rows, width_a)
        restored = restored.transpose(0, 1, 3, 2, 4).reshape(
            2, first_rows, second_rows, groups_b, width_b
        )
        regrouped = restored.transpose(0, 2, 3, 1, 4).reshape(
            2, second_rows, groups_b, first_rows * width_b
        )
        moved = complex_rows(
            second_prop, lax.all_to_all(regrouped, "rb", split_axis=2, concat_axis=1, tiled=True)
        )
        settled = lax.all_to_all(moved, "rb", split_axis=1, concat_axis=2, tiled=True)
        settled = settled.reshape(2, second_rows, groups_b, first_rows, width_b)
        amplitude = settled.transpose(0, 3, 1, 2, 4).reshape(2, first_rows, second_rows, channels)
    return amplitude


FAR_LEAD = 3


def flip(value, mask, bits):
    out = 0
    for n in range(bits):
        weight = 1 << n
        out = out + lax.rem(lax.div(value, weight) + lax.div(mask, weight), 2) * weight
    return out


def fused_kernel(ra, rb, amp_ref, coupling_ref, pattern_ref, turned_ref, first_ref, second_ref, upper,
                 lower, left, right, turn, stage, first_mat, second_mat, weights_ref, radial_ref, near, far, lines,
                 load_sem, send_sem, recv_near, recv_far, recv_back, recv_home, rad_send, rad_recv):
    at_a, at_b = lax.axis_index("ra"), lax.axis_index("rb")
    bits_a, bits_b = ra.bit_length() - 1, rb.bit_length() - 1
    chunks = left.shape[1]
    pairs = left.shape[2]
    sixteens = left.shape[4]
    groups = 2 * sixteens
    per = pairs * 2
    depth = first_ref.shape[1]
    halfway = lower.shape[1] // 2
    channels = lower.shape[4]
    a_tiles = lower.shape[2]
    devices = ra * rb
    route = [("b", bits_b - 1)] + [("b", n) for n in range(bits_b - 1)]
    route = route + [("a", n) for n in range(bits_a)]

    def partner(d):
        mask_a, mask_b = 0, 0
        for n, (axis, bit) in enumerate(route):
            one = lax.rem(lax.div(d, 1 << n), 2) * (1 << bit)
            if axis == "a":
                mask_a = mask_a + one
            else:
                mask_b = mask_b + one
        return flip(at_a, mask_a, bits_a), flip(at_b, mask_b, bits_b)

    barrier = pltpu.get_barrier_semaphore()

    def greet(d, carry):
        to_a, to_b = partner(devices - d)
        pl.semaphore_signal(barrier, inc=1, device_id=(to_a, to_b), device_id_type=MESH)
        return carry

    lax.fori_loop(1, devices, greet, 0)

    every_lane = pl.ds(0, channels)
    sheets = channels // LANES
    sheet = [pl.ds(s * LANES, LANES) for s in range(sheets)]
    last = chunks * pairs

    def edge(c):
        return (c == 0) | (c == last - 1)

    def spare(c, s):
        return last + lax.div(c, last - 1) * sheets + s

    def load(q):
        slot = lax.rem(q, 2)
        return pltpu.make_async_copy(amp_ref.at[:, :, pl.ds(q * TILE, TILE)], stage.at[slot], load_sem.at[slot])

    load(jnp.int32(0)).start()
    load(jnp.int32(1)).start()

    b_rows = amp_ref.shape[2]
    blocks = pattern_ref.shape[0]
    size_block = channels // blocks
    lane = lax.broadcasted_iota(jnp.int32, (size_block, channels), 1)
    for k in range(KTERMS):
        masked = []
        for i in range(blocks):
            keep = jnp.zeros((size_block, channels), jnp.float32)
            for j in range(blocks):
                inside = (lane >= j * size_block) & (lane < (j + 1) * size_block)
                keep = jnp.where(inside, pattern_ref[i, j, k].astype(jnp.float32), keep)
            masked.append(coupling_ref[k, i * size_block:(i + 1) * size_block].astype(jnp.float32) * keep)
        weights_ref[k] = jnp.transpose(jnp.concatenate(masked, axis=0)).astype(jnp.bfloat16)

    duos = KTERMS // 2
    for m in range(duos):
        radial_ref[m] = jnp.transpose(turned_ref[2 * m:2 * m + 2].reshape(2 * b_rows, radial_ref.shape[1]))

    def lay(g, carry):
        at = pl.ds(pl.multiple_of(g * HALF, HALF), HALF)
        near[g] = jnp.transpose(radial_ref[:, at].reshape(duos * HALF, 2 * b_rows))
        return carry

    lax.fori_loop(0, radial_ref.shape[1] // HALF, lay, 0)

    def kick(planes, factor_of, count):
        both = jnp.concatenate(planes, axis=0)
        total = [None, None]
        for k in range(KTERMS):
            applied = jnp.dot(both, weights_ref[k], preferred_element_type=jnp.float32)
            factor = factor_of(k)
            for p in range(2):
                term = applied[p * count:(p + 1) * count] * factor
                total[p] = term if k == 0 else total[p] + term
        return planes[0].astype(jnp.float32) + total[1], planes[1].astype(jnp.float32) - total[0]

    def kick_chunk(q, first=0, stop=None):
        slot = lax.rem(q, 2)
        if first == 0:
            load(q).wait()

        def group(g, carry):
            count = TILE * TILE
            planes = [stage[slot, p, pl.ds(g * TILE, TILE)].reshape(count, channels) for p in range(2)]
            laid = [[
                near[g * 2 + n, pl.ds(pl.multiple_of(odd * b_rows + q * TILE, TILE), TILE)] for n in range(2)
            ] for odd in range(2)]

            def factor_of(k):
                m, odd = divmod(k, 2)
                return jnp.concatenate([
                    jnp.broadcast_to(
                        laid[odd][n // HALF][:, m * HALF + n % HALF:m * HALF + n % HALF + 1], (TILE, channels)
                    ) for n in range(TILE)
                ], axis=0)

            result = kick(planes, factor_of, count)
            for p in range(2):
                turned = jnp.swapaxes(result[p].reshape(TILE, TILE, channels), 0, 1).astype(jnp.bfloat16)
                lower[p, pl.ds(q * TILE, TILE), g] = turned
            return carry

        lax.fori_loop(first, a_tiles if stop is None else stop, group, 0)
        if stop is None:
            @pl.when(q + 2 < chunks)
            def _():
                load(q + 2).start()

    def near_start(q, bp, d, first=0, count=None, lanes=every_lane, sem=None):
        to = flip(at_a, d, bits_a) if d < ra // 2 else opposite + d - ra // 2
        count = a_tiles if count is None else count
        source = lower.at[:, pl.ds(q * TILE + to * per + bp * 2, 2), pl.ds(first, count), :, lanes]
        target = left.at[:, q, bp, :, pl.ds(at_a * a_tiles + first, count), :, lanes]
        sem = recv_near.at[q * pairs + bp if sem is None else sem]
        if d == 0:
            pltpu.make_async_copy(source, target, sem).start()
        else:
            pltpu.make_async_remote_copy(
                src_ref=source, dst_ref=target, send_sem=send_sem.at[0], recv_sem=sem,
                device_id=(to, at_b), device_id_type=MESH,
            ).start()

    def home_start(q, bp, d, lanes=every_lane):
        to = flip(at_a, d, bits_a)
        source = right.at[:, q, bp, :, pl.ds(to * a_tiles, a_tiles), :, lanes]
        target = upper.at[:, pl.ds(q * TILE + at_a * per + bp * 2, 2), :, :, lanes]
        if d == 0:
            pltpu.make_async_copy(source, target, recv_home.at[q]).start()
        else:
            pltpu.make_async_remote_copy(
                src_ref=source, dst_ref=target, send_sem=send_sem.at[3], recv_sem=recv_home.at[q],
                device_id=(to, at_b), device_id_type=MESH,
            ).start()

    opposite = (1 - lax.div(at_a, ra // 2)) * (ra // 2)
    near_order = list(range(ra // 2, ra)) + list(range(1, ra // 2)) + [0]
    side = devices // 2

    def place(i, j, h):
        index = (i * rb + j) * 2 + h
        return lax.div(index, sixteens), lax.rem(index, sixteens)

    def far_start(c, h, crossing, lanes=every_lane):
        q, bp = lax.div(c, pairs), lax.rem(c, pairs)
        row = h * halfway + at_b * chunks + q
        target = upper.at[:, row, at_a * pairs + bp, :, lanes]

        def one(d, carry):
            to_a, to_b = partner(d)
            high, low = place(to_a, to_b, h)
            pltpu.make_async_remote_copy(
                src_ref=right.at[:, q, bp, high, low, :, lanes], dst_ref=target,
                send_sem=send_sem.at[1], recv_sem=recv_far.at[h], device_id=(to_a, to_b), device_id_type=MESH,
            ).start()
            return carry

        if crossing:
            lax.fori_loop(side, devices, one, 0)
        else:
            lax.fori_loop(1, side, one, 0)
            high, low = place(at_a, at_b, h)
            pltpu.make_async_copy(right.at[:, q, bp, high, low, :, lanes], target, recv_far.at[h]).start()

    def back_start(c, h, crossing, lanes=every_lane, sem=None):
        q, bp = lax.div(c, pairs), lax.rem(c, pairs)
        high, low = place(at_a, at_b, h)
        target = left.at[:, q, bp, high, low, :, lanes]
        sem = recv_back.at[c if sem is None else sem]

        def one(d, carry):
            to_a, to_b = partner(d)
            pltpu.make_async_remote_copy(
                src_ref=lower.at[:, h * halfway + to_b * chunks + q, to_a * pairs + bp, :, lanes], dst_ref=target,
                send_sem=send_sem.at[2], recv_sem=sem, device_id=(to_a, to_b), device_id_type=MESH,
            ).start()
            return carry

        if crossing:
            lax.fori_loop(side, devices, one, 0)
        else:
            lax.fori_loop(1, side, one, 0)
            pltpu.make_async_copy(
                lower.at[:, h * halfway + at_b * chunks + q, at_a * pairs + bp, :, lanes], target, sem
            ).start()

    def every(action):
        def one(c, carry):
            action(c)
            return carry

        lax.fori_loop(0, chunks * pairs, one, 0)

    def arrived(ref, sem):
        pltpu.make_async_copy(ref, ref, sem).wait()

    def first_chunk(c, lanes=every_lane, sem=None):
        q, bp = lax.div(c, pairs), lax.rem(c, pairs)
        arrived(left.at[:, q, bp, :, :, :, lanes], recv_near.at[c if sem is None else sem])
        made = []
        for par in range(2):
            both = jnp.concatenate([
                left[p, q, bp, par, :, :, lanes].reshape(depth, lanes.size) for p in range(2)
            ], axis=0)
            made.append(jnp.dot(first_mat[...], both, preferred_element_type=jnp.float32))
        for p in range(2):
            parts = [m[p * depth:(p + 1) * depth].reshape(groups, HALF, lanes.size) for m in made]
            mixed = jnp.concatenate(parts, axis=1).astype(jnp.bfloat16)
            right[p, q, bp, :, :, :, lanes] = mixed.reshape(2, sixteens, TILE, lanes.size)
        far_start(c, 0, False, lanes)
        far_start(c, 1, False, lanes)

    def last_chunk(c, lanes=every_lane):
        q, bp = lax.div(c, pairs), lax.rem(c, pairs)
        wide = [
            left[p, q, bp, :, :, :, lanes].reshape(groups, TILE, lanes.size).astype(jnp.float32) for p in range(2)
        ]
        for par in range(2):
            both = jnp.concatenate([
                w[:, par * HALF:(par + 1) * HALF].reshape(depth, lanes.size).astype(jnp.bfloat16) for w in wide
            ], axis=0)
            made = jnp.dot(first_mat[...], both, preferred_element_type=jnp.float32)
            for p in range(2):
                part = made[p * depth:(p + 1) * depth].reshape(sixteens, TILE, lanes.size)
                right[p, q, bp, par, :, :, lanes] = part.astype(jnp.bfloat16)
        for d in near_order:
            home_start(q, bp, d, lanes)

    def finish_chunk(q):
        arrived(upper.at[:, pl.ds(q * TILE, TILE)], recv_home.at[q])

        @pl.when(q < chunks - 1)
        def _():
            def group(g, carry):
                for p in range(2):
                    rows = upper[p, pl.ds(q * TILE, TILE), g].astype(jnp.float32)
                    upper[p, pl.ds(q * TILE, TILE), g] = jnp.swapaxes(rows, 0, 1).astype(jnp.bfloat16)
                return carry

            lax.fori_loop(0, a_tiles, group, 0)

    def near_all(q):
        for bp in range(pairs - 1):
            for d in near_order:
                near_start(q, bp, d)

        @pl.when(q < chunks - 1)
        def _():
            for d in near_order:
                near_start(q, pairs - 1, d)

        @pl.when(q == chunks - 1)
        def _():
            for s in range(sheets):
                for d in near_order:
                    near_start(q, pairs - 1, d, lanes=sheet[s], sem=spare(last - 1, s))

    start = jnp.int32(0)
    early = a_tiles * 3 // 4
    kick_chunk(start, 0, early)
    pl.semaphore_wait(barrier, devices - 1)
    for d in near_order:
        near_start(start, 0, d, 0, early, sheet[0], spare(start, 0))
    kick_chunk(start, early)
    for d in near_order:
        near_start(start, 0, d, early, a_tiles - early, sheet[0], spare(start, 0))
    for s in range(1, sheets):
        for d in near_order:
            near_start(start, 0, d, lanes=sheet[s], sem=spare(start, s))
    for bp in range(1, pairs):
        for d in near_order:
            near_start(start, bp, d)

    def rad_copy(n):
        to = flip(at_b, n, bits_b)
        return pltpu.make_async_remote_copy(
            src_ref=radial_ref.at[:, pl.ds(pl.multiple_of(to * TILE, TILE), TILE)], dst_ref=far.at[at_b],
            send_sem=rad_send, recv_sem=rad_recv, device_id=(at_a, to), device_id_type=MESH,
        )

    pltpu.make_async_copy(
        radial_ref.at[:, pl.ds(pl.multiple_of(at_b * TILE, TILE), TILE)], far.at[at_b], rad_recv
    ).start()

    def rad_start(n, carry):
        rad_copy(n).start()
        return carry

    lax.fori_loop(1, rb, rad_start, 0)

    for source, target in ((first_ref, first_mat), (second_ref, second_mat)):
        target[:depth, :depth] = source[0]
        target[depth:, depth:] = source[0]
        target[:depth, depth:] = -source[1]
        target[depth:, :depth] = source[1]

    def opening(t, carry):
        @pl.when(t < chunks)
        def _():
            kick_chunk(t)
            near_all(t)

        def one(c, carry):
            @pl.when(edge(c))
            def _():
                for s in range(sheets):
                    first_chunk(c, sheet[s], spare(c, s))

            @pl.when(jnp.logical_not(edge(c)))
            def _():
                first_chunk(c)

            return carry

        lax.fori_loop((t - 1) * pairs, t * pairs, one, 0)
        return carry

    lax.fori_loop(1, chunks + 1, opening, 0)
    def crossing(c, h):
        far_start(c, h, True)
        return h

    lax.fori_loop(0, chunks * pairs, crossing, 0)
    lax.fori_loop(0, FAR_LEAD, crossing, 1)

    arrived(lower.at[:, 0:lower.shape[1] * (ra - 1) // ra], send_sem.at[0])
    arrived(far, rad_recv)

    width = LANES
    block = a_tiles * TILE

    def middle(h, carry):
        arrived(upper.at[:, pl.ds(h * halfway, halfway)], recv_far.at[h])

        @pl.when(h == 0)
        def _():
            lax.fori_loop(FAR_LEAD, chunks * pairs, crossing, 1)

        pieces = far[:, :, pl.ds(pl.multiple_of(h * HALF, HALF), HALF)].reshape(rb * duos, HALF, 2 * b_rows)
        lines[...] = jnp.swapaxes(pieces, 0, 1)

        def spread(m, carry):
            for p in range(2):
                wide = upper[p, h * halfway + m].astype(jnp.float32).reshape(block, channels)
                for s in range(sheets):
                    turn[p, s, pl.ds(pl.multiple_of(m * block, block), block)] = wide[:, s * width:(s + 1) * width]
            return carry

        lax.fori_loop(0, halfway, spread, 0)

        def line(a, carry):
            size = second_ref.shape[1]
            at = pl.ds(a, size, stride=HALF)
            both = jnp.concatenate([
                jnp.concatenate([turn[p, s, at] for s in range(sheets)], axis=1).astype(jnp.bfloat16) for p in range(2)
            ], axis=0)
            made = jnp.dot(second_mat[...], both, preferred_element_type=jnp.float32).astype(jnp.bfloat16)
            laid = jnp.transpose(lines[a])

            def factor_of(k):
                m, odd = divmod(k, 2)
                half = laid[odd * b_rows:(odd + 1) * b_rows]
                return jnp.concatenate([
                    jnp.broadcast_to(half[:, n * duos + m:n * duos + m + 1], (b_rows, channels)) for n in range(rb)
                ], axis=0)

            kicked = kick([made[:size], made[size:]], factor_of, size)
            both = jnp.concatenate([x.astype(jnp.bfloat16) for x in kicked], axis=0)
            made = jnp.dot(second_mat[...], both, preferred_element_type=jnp.float32)
            for p in range(2):
                for s in range(sheets):
                    turn[p, s, at] = made[p * size:(p + 1) * size, s * width:(s + 1) * width]
            return carry

        lax.fori_loop(0, HALF, line, 0)

        def gather(m, carry):
            for p in range(2):
                wide = jnp.concatenate([
                    turn[p, s, pl.ds(pl.multiple_of(m * block, block), block)] for s in range(sheets)
                ], axis=1)
                lower[p, h * halfway + m] = wide.astype(jnp.bfloat16).reshape(a_tiles, TILE, channels)
            return carry

        lax.fori_loop(0, halfway, gather, 0)

        every(lambda c: back_start(c, h, True))
        return carry

    lax.fori_loop(0, 2, middle, 0)

    def part(c, s):
        @pl.when(edge(c))
        def _():
            for h in range(2):
                back_start(c, h, False, sheet[s], spare(c, s))

        @pl.when(jnp.logical_not(edge(c)))
        def _():
            back_start(c, s, False)

    part(jnp.int32(0), 0)
    part(jnp.int32(0), 1)
    part(jnp.int32(1), 0)
    arrived(right.at[:, :, :, :, 0:sixteens * (devices - 1) // devices], send_sem.at[1])

    def closing(t, carry):
        @pl.when(t < chunks)
        def _():
            def one(c, carry):
                bp = lax.rem(c, pairs)

                def onward():
                    @pl.when(c + 1 < last)
                    def _():
                        part(c + 1, 1)

                    @pl.when(c + 2 < last)
                    def _():
                        part(c + 2, 0)

                @pl.when(jnp.logical_not(edge(c)))
                def _():
                    arrived(left.at[:, t, bp], recv_back.at[c])
                    onward()
                    last_chunk(c)

                @pl.when(edge(c))
                def _():
                    arrived(left.at[:, t, bp, 0], recv_back.at[c])
                    for s in range(sheets):
                        arrived(left.at[:, t, bp, 0, :, :, sheet[s]], recv_back.at[spare(c, s)])
                        if s == sheets - 1:
                            onward()
                        last_chunk(c, sheet[s])

                return carry

            lax.fori_loop(t * pairs, (t + 1) * pairs, one, 0)

        @pl.when(t >= 1)
        def _():
            finish_chunk(t - 1)

        return carry

    lax.fori_loop(0, chunks + 1, closing, 0)

    arrived(lower.at[:, 0:lower.shape[1] * (devices - 1) // devices], send_sem.at[2])
    arrived(right.at[:, :, :, :, 0:sixteens * (ra - 1) // ra], send_sem.at[3])
    arrived(far.at[0:rb - 1], rad_send)


def unfold_kernel(in_ref, out_ref, stage, sem):
    tiles = stage.shape[1] // TILE
    done = in_ref.shape[1] // TILE - 1

    def ready(n, carry):
        q, g = lax.div(n, tiles), lax.rem(n, tiles)
        at = pl.ds(pl.multiple_of(q * TILE, TILE), TILE)
        pltpu.make_async_copy(in_ref.at[:, at, g], out_ref.at[:, pl.ds(g * TILE, TILE), at], sem).start()
        return carry

    lax.fori_loop(0, done * tiles, ready, 0)
    at = pl.ds(done * TILE, TILE)

    def group(g, carry):
        span = pl.ds(g * TILE, TILE)
        for p in range(2):
            turned = jnp.swapaxes(in_ref[p, at, g].astype(jnp.float32), 0, 1)
            stage[p, span] = turned.astype(jnp.bfloat16)
        pltpu.make_async_copy(stage.at[:, span], out_ref.at[:, span, at], sem).start()
        return carry

    lax.fori_loop(0, tiles, group, 0)
    pltpu.make_async_copy(in_ref, in_ref, sem).wait()


def unfold(folded, shape):
    return pl.pallas_call(
        unfold_kernel,
        in_specs=[pl.BlockSpec(memory_space=pltpu.VMEM)],
        out_specs=pl.BlockSpec(memory_space=pl.ANY),
        out_shape=jax.ShapeDtypeStruct(shape, jnp.bfloat16),
        scratch_shapes=[
            pltpu.VMEM((2, shape[1], TILE, shape[3]), jnp.bfloat16),
            pltpu.SemaphoreType.DMA(()),
        ],
        compiler_params=pltpu.CompilerParams(vmem_limit_bytes=16 * 2**20),
    )(folded)


def on_device(amplitude, coupling, pattern, radial, first_prop, second_prop):
    a_rows, b_rows, channels = amplitude.shape[1:]
    n_a, n_b = first_prop.shape[1], second_prop.shape[1]
    ra, rb = lax.axis_size("ra"), lax.axis_size("rb")
    devices = ra * rb
    chunks = b_rows // TILE
    fits = (
        channels == 2 * LANES and ra & (ra - 1) == 0 and rb == HALF and ra in (2, 4) and n_a == n_b
        and n_a == TILE * devices and n_b == TILE * devices and a_rows % TILE == 0 and b_rows % TILE == 0
        and chunks % 2 == 0 and chunks == ra and a_rows == TILE * HALF and 2 * b_rows == LANES and KTERMS % 2 == 0
    )
    if not fits:
        return plain(amplitude, coupling, pattern, radial, first_prop, second_prop)

    pairs = TILE // ra // 2
    groups = n_a // HALF
    flat = (2, chunks * TILE, a_rows // TILE, TILE, channels)
    tall = (2, chunks, pairs, 2, groups // 2, TILE, channels)
    whole = pl.BlockSpec(memory_space=pltpu.VMEM)
    kept = pl.BlockSpec(memory_space=pl.ANY)
    dma = pltpu.SemaphoreType.DMA
    folded = pl.pallas_call(
        functools.partial(fused_kernel, ra, rb),
        in_specs=[kept, whole, pl.BlockSpec(memory_space=pltpu.SMEM), whole, whole, whole],
        out_specs=whole,
        out_shape=pltpu.VMEM(flat, jnp.bfloat16),
        scratch_shapes=[
            pltpu.VMEM(flat, jnp.bfloat16),
            pltpu.VMEM(tall, jnp.bfloat16),
            pltpu.VMEM(tall, jnp.bfloat16),
            pltpu.VMEM((2, channels // LANES, n_b * HALF, LANES), jnp.float32),
            pltpu.VMEM((2, 2, a_rows, TILE, channels), jnp.bfloat16),
            pltpu.VMEM((2 * n_a, 2 * n_a), jnp.bfloat16),
            pltpu.VMEM((2 * n_b, 2 * n_b), jnp.bfloat16),
            pltpu.VMEM((KTERMS, channels, channels), jnp.bfloat16),
            pltpu.VMEM((KTERMS // 2, a_rows, 2 * b_rows), jnp.float32),
            pltpu.VMEM((a_rows // HALF, 2 * b_rows, KTERMS // 2 * HALF), jnp.float32),
            pltpu.VMEM((rb, KTERMS // 2, TILE, 2 * b_rows), jnp.float32),
            pltpu.VMEM((HALF, rb * KTERMS // 2, 2 * b_rows), jnp.float32),
            dma((2,)), dma((4,)), dma((chunks * pairs + 2 * channels // LANES,)), dma((2,)),
            dma((chunks * pairs + 2 * channels // LANES,)), dma((chunks,)),
            dma(()), dma(()),
        ],
        compiler_params=pltpu.CompilerParams(
            collective_id=0, has_side_effects=True, vmem_limit_bytes=55 * 2**20
        ),
    )(amplitude, coupling, pattern.transpose(1, 2, 0), radial.transpose(0, 2, 1), first_prop, second_prop)
    return unfold(folded, amplitude.shape)


def solution(mesh):
    return jax.shard_map(
        on_device,
        mesh=mesh,
        in_specs=(P(None, "ra", "rb", None), P(), P(), P(None, "ra", "rb"), P(), P()),
        out_specs=P(None, "ra", "rb", None),
        check_vma=False,
    )
```
